32 devices in a mesh: band: 8 (over z, y), col: 4 (over x, core).
Axes of the slice: x: 2, y: 2, z: 4, core: 2. Of those that a mesh axis runs over, the one named last changes fastest.
Arguments:
- demand: float32 [32768, 16], P(('band', 'col')), may hold values from -16 to 16
- lead_periods: int32 [32768], P(('band', 'col')), may hold values from 1 to 4
- matrix_tiles: float32 [8, 4, 128, 128, 128], P('band', 'col'), may hold values from -0.125 to 0.125
- tile_pos: int32 [8, 4, 128], P('band', 'col'), may hold values from 0 to 2047, as said below
- cost_vector: float32 [32768], P(('band', 'col')), may hold values from 0.05 to 7
- primal_init: float32 [32768, 16], P(('band', 'col')), may hold values from 0 to 2
- dual_init: float32 [32768, 16], P(('band', 'col')), may hold values from -6 to 6
- weight_init: float32 [16], replicated, may hold values from 0.5 to 2
Outputs:
- primal: float32 [32768, 16], P(('band', 'col'))
- dual_vars: float32 [32768, 16], P(('band', 'col'))
- weight: float32 [16], replicated
The draws below stay inside these ranges and needn't reach their ends.
Inputs may be any that keep to these rules, and one draw needn't show every extreme that they name: `tile_pos`: within one period and column block the 128 entries are different; entry v places its tile at row tile v // 64 of that period and column tile v % (64) of that column block.
All inputs are finite; a program needn't handle non-finite values.
Results may differ from the reference program's by a relative error of at most 0.0003.
Values sent between devices are 32-bit elements; how exact they have to be, the bound alone decides.
No kernel may reach another device: no remote copies, remote signals or barrier semaphores. Data moves between devices by JAX's collectives and lax.ppermute only.
A program may use at most 64 MiB of HBM per device.

```python
import math
import jax
import jax.numpy as jnp
from jax import lax

TILE = 128
PERIOD_ROWS = 4096
SCEN = 16
ITERS = 3
LEAD_MAX = 4
NT = 128
SUB = 8
SLOTS = 2048
ORDER = 32768
N_BAND = 8
N_COL = 4


def ramp_scales(key, count):
    position = jnp.arange(count, dtype=jnp.float32) / count
    ramp_factor = 1.0 + 2.0 * position
    rough_part = jnp.exp(jax.random.uniform(key, (count,), jnp.float32, jnp.log(0.3), jnp.log(3.0)))
    return ramp_factor * rough_part


def draw_demand(key, part):
    key_scale = jax.random.fold_in(key, 11)
    key_body = jax.random.fold_in(key, 12)
    scales = ramp_scales(key_scale, ORDER)[:, None]
    return 0.5 * scales * jax.random.truncated_normal(key_body, -3.0, 3.0, (ORDER, SCEN), jnp.float32)


def draw_cost_vector(key, part):
    key_scale = jax.random.fold_in(key, 21)
    scales = ramp_scales(key_scale, ORDER)
    return 0.5 * scales


def draw_tile_pos(key, part):
    key_list = jax.random.split(jax.random.fold_in(key, 31), N_BAND * N_COL)

    def one_device(device_key):
        return jax.random.permutation(device_key, SLOTS)[:NT].astype(jnp.int32)
    return jax.vmap(one_device)(key_list).reshape(N_BAND, N_COL, NT)


def plant(values, rng, least, high):
    longest = values.shape.index(max(values.shape))
    spots = []
    for shift in (0, 1):
        where = [jax.random.randint(jax.random.fold_in(rng, axis), (), 0, length) for axis, length in enumerate(values.shape)]
        where[longest] = (where[longest] + shift) % values.shape[longest]
        spots.append(tuple(where))
    return values.at[spots[0]].set(least).at[spots[1]].set(high)


def level_of(stream_key, shape, cuts, smallest, high):
    factor_of = 1.0
    for axis_at, parts in cuts:
        heights = jax.random.uniform(jax.random.fold_in(jax.random.fold_in(stream_key, 6), axis_at), (parts,), jnp.float32, smallest / len(cuts), high / len(cuts))
        factor_of = factor_of * jnp.repeat(jnp.exp(heights), shape[axis_at] // parts).reshape((-1,) + (1,) * (len(shape) - 1 - axis_at))
    return factor_of


def gaussian(rng, shape, width, limit, pieces=(), held_as=jnp.bfloat16):
    level = level_of(rng, shape, pieces, -0.22, 0.18) if pieces else 1.0
    array = jax.random.normal(rng, shape, jnp.float32) * width * level
    return jnp.minimum(jnp.maximum(array, -limit), limit).astype(held_as)


def setup_inputs(seed: int = 0) -> dict:
    key_of = jax.random.split(jax.random.key(seed), 9)
    return {
        "demand": draw_demand(jax.random.fold_in(key_of[8], 71), 0),
        "lead_periods": plant(jax.random.randint(key_of[1], (ORDER,), 1, LEAD_MAX + 1), jax.random.fold_in(key_of[1], 1), 1, LEAD_MAX).astype(jnp.int32),
        "matrix_tiles": gaussian(key_of[2], (N_BAND, N_COL, NT, TILE, TILE), (NT * TILE // SUB) ** -0.5, 0.125, ((0, 8), (1, 4)), jnp.float32),
        "tile_pos": draw_tile_pos(jax.random.fold_in(key_of[8], 71), 0),
        "cost_vector": draw_cost_vector(jax.random.fold_in(key_of[8], 71), 0),
        "primal_init": jnp.clip(2.0 * jax.random.uniform(key_of[5], (ORDER, SCEN), jnp.float32) ** level_of(key_of[5], (ORDER, SCEN), ((0, 32),), -0.2, 0.2), 0.0, 2.0),
        "dual_init": gaussian(key_of[6], (ORDER, SCEN), 1.0, 6.0, ((0, 32),), jnp.float32),
        "weight_init": jnp.clip(jnp.exp(jax.random.uniform(key_of[7], (SCEN,), jnp.float32, math.log(0.5), math.log(2.0))), 0.5, 2.0),
    }


step_scale = 0.45
return_share = 0.6
epsilon = 1e-06
highest = lax.Precision.HIGHEST

def apply_matrix(matrix_tiles, tile_pos, field):
    units_col = N_BAND * SUB
    units_row = N_COL * SUB
    field_grid = field.reshape(N_BAND, N_COL, SUB, TILE, SCEN)
    col_units = jnp.transpose(field_grid, (1, 0, 2, 3, 4)).reshape(N_COL, units_col, TILE, SCEN)
    column_ids = jnp.arange(N_COL, dtype=jnp.int32)[:, None]

    def one_band(inputs):
        band_tiles, band_pos = inputs
        picked = col_units[column_ids, band_pos % units_col]
        product = jnp.einsum('qtij,qtjs->qtis', band_tiles, picked, precision=highest)
        onehot = (band_pos[:, :, None] // units_col == jnp.arange(units_row, dtype=jnp.int32)[None, None, :]).astype(jnp.float32)
        return jnp.einsum('qtr,qtis->ris', onehot, product, precision=highest)
    result = lax.map(one_band, (matrix_tiles, tile_pos))
    return result.reshape(ORDER, SCEN)

def apply_transpose(matrix_tiles, tile_pos, dual_vars):
    units_col = N_BAND * SUB
    units_row = N_COL * SUB
    dual_grid = dual_vars.reshape(N_BAND, units_row, TILE, SCEN)
    column_ids = jnp.arange(N_COL, dtype=jnp.int32)[:, None]

    def one_band(running, inputs):
        band_tiles, band_pos, band_dual = inputs
        picked = band_dual[band_pos // units_col]
        product = jnp.einsum('qtij,qtis->qtjs', band_tiles, picked, precision=highest)
        running = running.at[column_ids, band_pos % units_col].add(product)
        return (running, None)
    start = jnp.zeros((N_COL, units_col, TILE, SCEN), jnp.float32)
    running, unused = lax.scan(one_band, start, (matrix_tiles, tile_pos, dual_grid))
    running = running.reshape(N_COL, N_BAND, SUB, TILE, SCEN)
    return jnp.transpose(running, (1, 0, 2, 3, 4)).reshape(ORDER, SCEN)

def reference(demand, lead_periods, matrix_tiles, tile_pos, cost_vector, primal_init, dual_init, weight_init):
    demand_grid = demand.reshape(N_BAND, PERIOD_ROWS, SCEN)
    lead_grid = lead_periods.reshape(N_BAND, PERIOD_ROWS, 1)
    lagged = jnp.zeros((N_BAND, PERIOD_ROWS, SCEN), jnp.float32)
    for lead in range(1, LEAD_MAX + 1):
        lagged = jnp.where(lead_grid == lead, jnp.roll(demand_grid, lead, axis=0), lagged)
    right_side = (demand_grid - return_share * lagged).reshape(ORDER, SCEN)
    primal = primal_init
    dual_vars = dual_init
    weight = weight_init
    for iteration in range(ITERS):
        primal_step = step_scale / weight
        dual_step = step_scale * weight
        pull_terms = apply_transpose(matrix_tiles, tile_pos, dual_vars)
        primal_new = jnp.maximum(primal - primal_step[None, :] * (cost_vector[:, None] - pull_terms), 0.0)
        push_terms = apply_matrix(matrix_tiles, tile_pos, 2.0 * primal_new - primal)
        dual_new = dual_vars + dual_step[None, :] * (right_side - push_terms)
        primal_change = primal_new - primal
        dual_change = dual_new - dual_vars
        primal_square = lax.optimization_barrier(jnp.sum(primal_change * primal_change, axis=0))
        dual_square = lax.optimization_barrier(jnp.sum(dual_change * dual_change, axis=0))
        weight = jnp.sqrt(weight * jnp.sqrt((primal_square + epsilon) / (dual_square + epsilon)))
        primal = primal_new
        dual_vars = dual_new
    return (primal, dual_vars, weight)
```

```python
import jax
import jax.numpy as jnp
from jax import lax
from jax.experimental import pallas as pl
from jax.experimental.pallas import tpu as pltpu
from jax.sharding import PartitionSpec as P

ITERS = 3
LEAD_MAX = 4
GROUP = 32

step_scale = 0.45
return_share = 0.6
epsilon = 1e-06
F32 = jnp.float32
BF16 = jnp.bfloat16


def bit_count(count):
    bits = count.bit_length() - 1
    assert count == 1 << bits and bits >= 2
    return bits


def bit_position(relative, order):
    bits = len(order)
    place = 0
    for step, bit in enumerate(order):
        place = place + (((relative >> bit) & 1) << (bits - 1 - step))
    return place


def exchanged(value, axis, mask):
    count = lax.axis_size(axis)
    return lax.ppermute(value, axis, [(source, source ^ mask) for source in range(count)])


def passed_along(value, axis, steps):
    count = lax.axis_size(axis)
    return lax.ppermute(value, axis, [(source, (source + steps) % count) for source in range(count)])


def halves(value):
    high = value.astype(BF16)
    low = (value - high.astype(F32)).astype(BF16)
    return high, low


def stacked(value):
    high, low = halves(value)
    return jnp.concatenate(
        [jnp.concatenate([high, high], 1), jnp.concatenate([low, low], 1)], 0
    )


def whole_spec(array):
    rank = len(array.shape)
    return pl.BlockSpec(array.shape, lambda step, *refs: (0,) * rank)


def call_once(body, inputs, outputs):
    return pl.pallas_call(
        body, out_shape=[jax.ShapeDtypeStruct(shape, F32) for shape in outputs]
    )(*inputs)


def to_units(block, tile):
    return [block[:, k * tile : (k + 1) * tile] for k in range(block.shape[1] // tile)]


def prepare(dual_rows, primal_rows, cost, tile):
    scen, rows = dual_rows.shape
    sub = rows // tile

    def body(dual_ref, primal_ref, cost_ref, units_ref, message_ref):
        for k in range(sub):
            lanes = slice(k * tile, (k + 1) * tile)
            units_ref[k] = dual_ref[:, lanes]
            message_ref[k] = primal_ref[:, lanes]
        message_ref[sub] = jnp.zeros((scen, tile), F32)
        message_ref[sub, :sub, :] = cost_ref[...]

    return call_once(
        body,
        (dual_rows, primal_rows, cost),
        ((sub, scen, tile), (sub + 1, scen, tile)),
    )


def right_side_of(demand_rows, earlier, lead, tile):
    scen, rows = demand_rows.shape
    sub = rows // tile

    def body(demand_ref, *refs):
        lead_ref, out_ref = refs[-2:]
        for k in range(sub):
            lanes = slice(k * tile, (k + 1) * tile)
            wanted = lead_ref[k : k + 1, :]
            lagged = jnp.zeros((scen, tile), F32)
            for steps in range(1, LEAD_MAX + 1):
                lagged = jnp.where(wanted == steps, refs[steps - 1][:, lanes], lagged)
            out_ref[k] = demand_ref[:, lanes] - return_share * lagged

    return call_once(body, (demand_rows, *earlier, lead), ((sub, scen, tile),))[0]


def backward_kernel(index, own, other, matrix_tiles, order_a, order_b, sub):
    count, tile, _ = matrix_tiles.shape
    scen = own.shape[1]
    half_scen = scen // 2
    per_half = own.shape[0] - 1
    chunks = 1 << len(order_a)
    units = chunks * sub
    half = units // 2
    group = min(GROUP, count)

    def body(index_ref, own_ref, other_ref, tiles_ref, *refs):
        send_a, keep_a, send_b, keep_b, total, operand = refs
        step = pl.program_id(0)

        @pl.when(step == 0)
        def _():
            total[...] = jnp.zeros_like(total)
            for u in range(per_half):
                operand[u] = stacked(own_ref[u])
                operand[per_half + u] = stacked(other_ref[u])

        for k in range(group):
            t = step * group + k
            row = index_ref[t]
            column = index_ref[count + t]
            high, low = halves(tiles_ref[k])
            product = lax.dot_general(
                operand[row],
                jnp.concatenate([high, low], 0),
                (((1,), (0,)), ((), ())),
                preferred_element_type=F32,
            )
            total[column] += product[:scen] + product[scen:]

        @pl.when(step == pl.num_programs(0) - 1)
        def _():
            for relative in range(chunks):
                place_a = bit_position(relative, order_a) * sub
                place_b = bit_position(relative, order_b) * sub
                for k in range(sub):
                    value = total[place_a + k]
                    for place, send, keep, part in (
                        (place_a + k, send_a, keep_a, value[:half_scen]),
                        (place_b + k, send_b, keep_b, value[half_scen:]),
                    ):
                        if place >= half:
                            send[place - half] = part
                        else:
                            keep[place] = part
            square = own_ref[per_half] + other_ref[per_half]
            send_a[half] = square[:half_scen]
            send_b[half] = square[half_scen:]

    shapes = [(half + 1, half_scen, tile), (half, half_scen, tile)] * 2
    outs = [jax.ShapeDtypeStruct(shape, F32) for shape in shapes]
    return pl.pallas_call(
        body,
        out_shape=outs,
        grid_spec=pltpu.PrefetchScalarGridSpec(
            num_scalar_prefetch=1,
            grid=(count // group,),
            in_specs=[
                whole_spec(own),
                whole_spec(other),
                pl.BlockSpec((group, tile, tile), lambda step, refs: (step, 0, 0)),
            ],
            out_specs=[whole_spec(out) for out in outs],
            scratch_shapes=[
                pltpu.VMEM((units, scen, tile), F32),
                pltpu.VMEM((2 * per_half, 2 * scen, 2 * tile), BF16),
            ],
        ),
        compiler_params=pltpu.CompilerParams(dimension_semantics=("arbitrary",)),
    )(index, own, other, matrix_tiles)


def forward_kernel(index, parts, matrix_tiles, order_a, order_b, units_row, sub):
    count, tile, _ = matrix_tiles.shape
    half_scen = parts[0].shape[1]
    scen = 2 * half_scen
    per_half = parts[0].shape[0] - 1
    chunks = 1 << len(order_a)
    half = units_row // 2
    group = min(GROUP, count)

    def body(index_ref, own_a, other_a, own_b, other_b, tiles_ref, *refs):
        send, keep, total, operand = refs
        step = pl.program_id(0)

        def unit(own, other, place):
            return other[place - per_half] if place >= per_half else own[place]

        @pl.when(step == 0)
        def _():
            total[...] = jnp.zeros_like(total)
            for relative in range(chunks):
                place_a = bit_position(relative, order_a) * sub
                place_b = bit_position(relative, order_b) * sub
                for k in range(sub):
                    value = jnp.concatenate(
                        [unit(own_a, other_a, place_a + k), unit(own_b, other_b, place_b + k)], 0
                    )
                    operand[place_a + k] = stacked(value)

        for k in range(group):
            t = step * group + k
            row = index_ref[t]
            column = index_ref[count + t]
            high, low = halves(tiles_ref[k])
            product = lax.dot_general(
                operand[column],
                jnp.concatenate([high, low], 1),
                (((1,), (1,)), ((), ())),
                preferred_element_type=F32,
            )
            total[row] += product[:scen] + product[scen:]

        @pl.when(step == pl.num_programs(0) - 1)
        def _():
            for u in range(half):
                keep[u] = total[u]
                send[u] = total[half + u]
            send[half, :half_scen, :] = own_a[per_half] + other_a[per_half]
            send[half, half_scen:, :] = own_b[per_half] + other_b[per_half]

    outs = [
        jax.ShapeDtypeStruct((half + 1, scen, tile), F32),
        jax.ShapeDtypeStruct((half, scen, tile), F32),
    ]
    return pl.pallas_call(
        body,
        out_shape=outs,
        grid_spec=pltpu.PrefetchScalarGridSpec(
            num_scalar_prefetch=1,
            grid=(count // group,),
            in_specs=[whole_spec(part) for part in parts]
            + [pl.BlockSpec((group, tile, tile), lambda step, refs: (step, 0, 0))],
            out_specs=[whole_spec(out) for out in outs],
            scratch_shapes=[
                pltpu.VMEM((units_row, scen, tile), F32),
                pltpu.VMEM((chunks * sub, 2 * scen, 2 * tile), BF16),
            ],
        ),
        compiler_params=pltpu.CompilerParams(dimension_semantics=("arbitrary",)),
    )(index, *parts, matrix_tiles)


def next_weight(weight, primal_square, dual_square):
    primal_sum = jnp.sum(primal_square, axis=-1, keepdims=True)
    dual_sum = jnp.sum(dual_square, axis=-1, keepdims=True)
    ratio = (primal_sum + epsilon) / (dual_sum + epsilon)
    return jnp.sqrt(weight * jnp.sqrt(ratio))


def primal_update(own, other, start_own, start_other, primal, weight, primal_square, sub, last):
    _, scen, tile = own.shape
    half_scen = scen // 2
    first = primal is None

    def body(*refs):
        refs = list(refs)
        own_ref, other_ref, start_refs = refs[0], refs[1], refs[2:4]
        weight_ref = refs[4]
        rest = refs[5:]
        if not first:
            primal_ref, square_ref = rest[:2]
            rest = rest[2:]
        new_ref, message_a, message_b = rest[:3]
        rest = rest[3:]
        weight_now = weight_ref[...]
        if not first:
            weight_now = next_weight(
                weight_now, square_ref[...], own_ref[2 * sub] + other_ref[2 * sub]
            )
            rest[0][...] = weight_now
            rest = rest[1:]
        primal_step = step_scale / weight_now
        squares = []
        for chunk in range(2):
            square = jnp.zeros((scen, tile), F32)
            for k in range(sub):
                here = chunk * sub + k
                pull = own_ref[here] + other_ref[(1 - chunk) * sub + k]
                before = start_refs[chunk][k] if first else primal_ref[here]
                cost = start_refs[chunk][sub, k : k + 1, :]
                after = jnp.maximum(before - primal_step * (cost - pull), 0.0)
                change = after - before
                square = square + change * change
                new_ref[here] = after
                ahead = 2.0 * after - before
                message_a[here] = ahead[:half_scen]
                message_b[here] = ahead[half_scen:]
                if last and chunk == 0:
                    rest[0][:, k * tile : (k + 1) * tile] = after
            squares.append(square)
        square = squares[0] + squares[1]
        message_a[2 * sub] = square[:half_scen]
        message_b[2 * sub] = square[half_scen:]

    inputs = [own, other, start_own, start_other, weight]
    outputs = [(2 * sub, scen, tile)] + [(2 * sub + 1, half_scen, tile)] * 2
    if not first:
        inputs += [primal, primal_square]
        outputs.append((scen, tile))
    if last:
        outputs.append((scen, sub * tile))
    return call_once(body, inputs, outputs)


def dual_update(own, other, duals, rights, weight, sub, last):
    _, scen, tile = own.shape
    pair = isinstance(duals, tuple)
    given = list(duals) if pair else [duals]

    def body(*refs):
        refs = list(refs)
        own_ref, other_ref, weight_ref = refs[:3]
        right_refs = refs[3:5]
        dual_refs = refs[5 : 5 + len(given)]
        rest = refs[5 + len(given) :]
        message, square_ref = rest[:2]
        square_ref[...] = own_ref[2 * sub] + other_ref[2 * sub]
        dual_step = step_scale * weight_ref[...]
        squares = []
        for chunk in range(2):
            square = jnp.zeros((scen, tile), F32)
            for k in range(sub):
                here = chunk * sub + k
                push = own_ref[here] + other_ref[(1 - chunk) * sub + k]
                before = dual_refs[chunk][k] if pair else dual_refs[0][here]
                after = before + dual_step * (right_refs[chunk][k] - push)
                change = after - before
                square = square + change * change
                message[here] = after
                if last and chunk == 0:
                    rest[2][:, k * tile : (k + 1) * tile] = after
            squares.append(square)
        message[2 * sub] = squares[0] + squares[1]

    outputs = [(2 * sub + 1, scen, tile), (scen, tile)]
    if last:
        outputs.append((scen, sub * tile))
    return call_once(body, [own, other, weight, *rights, *given], outputs)


def folded(send, keep, received):
    return keep + received[:-1], send[-1:] + received[-1:]


def on_device(
    demand, lead_periods, matrix_tiles, tile_pos, cost_vector, primal_init, dual_init, weight_init
):
    band_bits = bit_count(lax.axis_size("band"))
    col_bits = bit_count(lax.axis_size("col"))
    assert col_bits == 2
    matrix_tiles = matrix_tiles.reshape(matrix_tiles.shape[2:])
    positions = tile_pos.reshape(-1)
    tile = matrix_tiles.shape[-1]
    block_rows, scen = demand.shape
    sub = block_rows // tile
    units_col = sub << band_bits
    units_row = sub << col_bits
    order_a = tuple(range(band_bits))
    order_b = (1, 0) + order_a[2:]
    order_col = tuple(range(col_bits))

    def place_of(unit, axis, order):
        relative = (unit // sub) ^ lax.axis_index(axis)
        return bit_position(relative, order) * sub + unit % sub

    index = jnp.concatenate(
        [
            place_of(positions // units_col, "col", order_col),
            place_of(positions % units_col, "band", order_a),
        ]
    )
    demand_rows = demand.T
    dual_units, start_own = prepare(
        dual_init.T, primal_init.T, cost_vector.reshape(sub, tile), tile
    )
    dual_other = exchanged(dual_units, "col", 1 << order_col[-1])
    message = jnp.concatenate([dual_units, dual_other, jnp.zeros((1, scen, tile), F32)])
    start_other = exchanged(start_own, "band", 1 << order_a[-1])
    earlier = [passed_along(demand_rows, "band", steps) for steps in range(1, LEAD_MAX + 1)]
    right_own = right_side_of(demand_rows, earlier, lead_periods.reshape(sub, tile), tile)
    right_other = exchanged(right_own, "col", 1 << order_col[-1])
    duals = (dual_units, dual_other)
    weight = jnp.broadcast_to(weight_init[:, None], (scen, tile))
    primal = None
    primal_square = None
    for iteration in range(ITERS):
        last = iteration == ITERS - 1
        other = exchanged(message, "col", 1 << order_col[0])
        send_a, keep_a, send_b, keep_b = backward_kernel(
            index, message, other, matrix_tiles, order_a, order_b, sub
        )
        got_a = exchanged(send_a, "band", 1 << order_a[0])
        got_b = exchanged(send_b, "band", 1 << order_b[0])
        sides = []
        for order, send, keep, got in (
            (order_a, send_a, keep_a, got_a),
            (order_b, send_b, keep_b, got_b),
        ):
            total, square = folded(send, keep, got)
            half = total.shape[0] // 2
            sides.append((order[1], jnp.concatenate([total[half:], square]), total[:half]))
        sides = [
            folded(send, keep, exchanged(send, "band", 1 << bit)) for bit, send, keep in sides
        ]
        total, square = (jnp.concatenate(pair, 1) for pair in zip(*sides))
        for bit in order_a[2:-1]:
            half = total.shape[0] // 2
            send, keep = jnp.concatenate([total[half:], square]), total[:half]
            total, square = folded(send, keep, exchanged(send, "band", 1 << bit))
        own = jnp.concatenate([total, square])
        results = primal_update(
            own,
            exchanged(own, "band", 1 << order_a[-1]),
            start_own,
            start_other,
            primal,
            weight,
            primal_square,
            sub,
            last,
        )
        primal, ahead_a, ahead_b = results[:3]
        if iteration:
            weight = results[3]
        if last:
            primal_rows = results[-1]
        ahead = [ahead_a, ahead_b]
        for place in range(band_bits - 2, 0, -1):
            joined = []
            for order, own in zip((order_a, order_b), ahead):
                got = exchanged(own, "band", 1 << order[place])
                joined.append(
                    jnp.concatenate([own[:-1], got[:-1], own[-1:] + got[-1:]])
                )
            ahead = joined
        parts = []
        for order, own in zip((order_a, order_b), ahead):
            parts += [own, exchanged(own, "band", 1 << order[0])]
        send, keep = forward_kernel(index, parts, matrix_tiles, order_a, order_b, units_row, sub)
        total, square = folded(send, keep, exchanged(send, "col", 1 << order_col[0]))
        own = jnp.concatenate([total, square])
        results = dual_update(
            own,
            exchanged(own, "col", 1 << order_col[1]),
            duals,
            (right_own, right_other),
            weight,
            sub,
            last,
        )
        message, primal_square = results[:2]
        duals = message
        if last:
            dual_rows = results[2]
    square = message[-1]
    square = square + exchanged(square, "col", 1 << order_col[0])
    for bit in order_a:
        square = square + exchanged(square, "band", 1 << bit)
    weight = next_weight(weight, primal_square, square)[:, 0]
    return (primal_rows.T, dual_rows.T, weight)


def solution(mesh):
    in_specs = (
        P(("band", "col"), None),
        P(("band", "col")),
        P("band", "col", None, None, None),
        P("band", "col", None),
        P(("band", "col")),
        P(("band", "col"), None),
        P(("band", "col"), None),
        P(),
    )
    out_specs = (P(("band", "col"), None), P(("band", "col"), None), P())
    return jax.shard_map(
        on_device, mesh=mesh, in_specs=in_specs, out_specs=out_specs, check_vma=False
    )
```

```python
import jax
import jax.numpy as jnp
from jax import lax
from jax.experimental import pallas as pl
from jax.experimental.pallas import tpu as pltpu
from jax.sharding import PartitionSpec as P

ITERS = 3
LEAD_MAX = 4
GROUP = 32
PIECE = 16

step_scale = 0.45
return_share = 0.6
epsilon = 1e-06
F32 = jnp.float32
BF16 = jnp.bfloat16


def bit_count(count):
    bits = count.bit_length() - 1
    assert count == 1 << bits and bits >= 2
    return bits


def bit_position(relative, order):
    bits = len(order)
    place = 0
    for step, bit in enumerate(order):
        place = place + (((relative >> bit) & 1) << (bits - 1 - step))
    return place


def exchanged(value, axis, mask):
    count = lax.axis_size(axis)
    return lax.ppermute(value, axis, [(source, source ^ mask) for source in range(count)])


def passed_along(value, axis, steps):
    count = lax.axis_size(axis)
    return lax.ppermute(value, axis, [(source, (source + steps) % count) for source in range(count)])


def halves(value):
    high = value.astype(BF16)
    low = (value - high.astype(F32)).astype(BF16)
    return high, low


def stacked(value):
    high, low = halves(value)
    return jnp.concatenate(
        [jnp.concatenate([high, high], 1), jnp.concatenate([low, low], 1)], 0
    )


def call_once(body, inputs, outputs):
    return pl.pallas_call(
        body, out_shape=[jax.ShapeDtypeStruct(shape, F32) for shape in outputs]
    )(*inputs)


def unit_of(ref, k, tile):
    return ref[:, k * tile : (k + 1) * tile] if len(ref.shape) == 2 else ref[k]


def tile_products(index, parts, matrix_tiles, transposed, operand_units, total_units, sub, finish, extra, outputs):
    count, tile, _ = matrix_tiles.shape
    scen = parts[0].shape[-2]
    group = min(GROUP, count)
    piece = min(PIECE, group)
    pieces = count // piece

    def body(index_ref, tiles_ref, *refs):
        part_refs = refs[: len(parts)]
        extra_refs = refs[len(parts) : len(parts) + len(extra)]
        out_refs = refs[len(parts) + len(extra) : -4]
        held, total, operand, arrived = refs[-4:]

        def copy_of(which):
            where = pl.ds(which * piece, piece)
            return pltpu.make_async_copy(tiles_ref.at[where], held.at[where], arrived.at[which])

        for which in range(pieces):
            copy_of(which).start()
        total[...] = jnp.zeros_like(total)
        per_part = operand_units // len(parts)
        for which, ref in enumerate(part_refs):
            for k in range(per_part):
                operand[which * per_part + k] = stacked(unit_of(ref, k, tile))

        def one_group(step, carry):
            for k in range(group):
                if k % piece == 0:
                    copy_of(step * (group // piece) + k // piece).wait()
                t = step * group + k
                row = index_ref[t]
                column = index_ref[count + t]
                high, low = halves(held[t])
                if transposed:
                    operand_at, weights, sides, total_at = (
                        row,
                        jnp.concatenate([high, low], 0),
                        (((1,), (0,)), ((), ())),
                        column,
                    )
                else:
                    operand_at, weights, sides, total_at = (
                        column,
                        jnp.concatenate([high, low], 1),
                        (((1,), (1,)), ((), ())),
                        row,
                    )
                product = lax.dot_general(
                    operand[operand_at], weights, sides, preferred_element_type=F32
                )
                total[total_at] += product[:scen] + product[scen:]
            return carry

        lax.fori_loop(0, count // group, one_group, 0)
        finish(part_refs, extra_refs, total, out_refs)

    in_vmem = pl.BlockSpec(memory_space=pltpu.VMEM)
    return pl.pallas_call(
        body,
        out_shape=[jax.ShapeDtypeStruct(shape, F32) for shape in outputs],
        in_specs=[
            pl.BlockSpec(memory_space=pltpu.SMEM),
            pl.BlockSpec(memory_space=pl.ANY),
        ]
        + [in_vmem] * (len(parts) + len(extra)),
        out_specs=[in_vmem] * len(outputs),
        scratch_shapes=[
            pltpu.VMEM((count, tile, tile), F32),
            pltpu.VMEM((total_units, scen, tile), F32),
            pltpu.VMEM((operand_units, 2 * scen, 2 * tile), BF16),
            pltpu.SemaphoreType.DMA((pieces,)),
        ],
    )(index, matrix_tiles, *parts, *extra)


def backward_product(index, parts, matrix_tiles, units_row, units_col, sub):
    scen, tile = parts[0].shape[-2], matrix_tiles.shape[-1]
    quarter = units_col // 4
    carried = len(parts) == 2

    def finish(part_refs, extra_refs, total, out_refs):
        for mask in range(4):
            for k in range(quarter):
                out_refs[mask][k] = total[mask * quarter + k]
        if carried:
            square = part_refs[0][units_row // 2] + part_refs[1][units_row // 2]
        else:
            square = jnp.zeros((scen, tile), F32)
        for mask in range(4):
            out_refs[mask][quarter] = square

    return tile_products(
        index, parts, matrix_tiles, True, units_row, units_col, sub, finish, [],
        [(quarter + 1, scen, tile)] * 4,
    )


def forward_product(index, parts, matrix_tiles, right_side, units_row, units_col, sub):
    _, scen, tile = parts[0].shape
    quarter = units_col // 4
    half = units_row // 2

    def finish(part_refs, extra_refs, total, out_refs):
        keep, send = out_refs
        for k in range(half):
            value = total[k]
            keep[k] = value - extra_refs[0][k] if k < sub else value
            send[k] = total[half + k]
        squares = [ref[quarter] for ref in part_refs]
        square = (squares[0] + squares[1]) + (squares[2] + squares[3])
        keep[half] = square
        send[half] = square

    return tile_products(
        index, parts, matrix_tiles, False, units_col, units_row, sub, finish, [right_side],
        [(half + 1, scen, tile)] * 2,
    )


def right_side_of(demand_rows, earlier, lead, tile):
    scen, rows = demand_rows.shape
    sub = rows // tile

    def body(demand_ref, *refs):
        lead_ref, out_ref = refs[-2:]
        for k in range(sub):
            lanes = slice(k * tile, (k + 1) * tile)
            wanted = lead_ref[k : k + 1, :]
            lagged = jnp.zeros((scen, tile), F32)
            for steps in range(1, LEAD_MAX + 1):
                lagged = jnp.where(wanted == steps, refs[steps - 1][:, lanes], lagged)
            out_ref[k] = demand_ref[:, lanes] - return_share * lagged

    return call_once(body, (demand_rows, *earlier, lead), ((sub, scen, tile),))[0]


def next_weight(weight, primal_square, dual_square):
    primal_sum = jnp.sum(primal_square, axis=-1, keepdims=True)
    dual_sum = jnp.sum(dual_square, axis=-1, keepdims=True)
    ratio = (primal_sum + epsilon) / (dual_sum + epsilon)
    return jnp.sqrt(weight * jnp.sqrt(ratio))


def primal_update(own, other, starts, primal, weight, primal_square, sub, last):
    _, scen, tile = own.shape
    first = primal is None

    def body(*refs):
        own_ref, other_ref = refs[:2]
        start_refs = refs[2:4]
        weight_ref = refs[4]
        rest = refs[5:]
        if not first:
            primal_ref, square_ref = rest[:2]
            rest = rest[2:]
        new_ref, message = rest[:2]
        rest = rest[2:]
        weight_now = weight_ref[...]
        if not first:
            weight_now = next_weight(
                weight_now, square_ref[...], own_ref[2 * sub] + other_ref[2 * sub]
            )
            rest[0][...] = weight_now
            rest = rest[1:]
        primal_step = step_scale / weight_now
        squares = []
        for chunk in range(2):
            square = jnp.zeros((scen, tile), F32)
            for k in range(sub):
                here = chunk * sub + k
                lanes = slice(k * tile, (k + 1) * tile)
                pull = own_ref[here] + other_ref[(1 - chunk) * sub + k]
                before = start_refs[chunk][:scen, lanes] if first else primal_ref[here]
                cost = start_refs[chunk][scen : scen + 1, lanes]
                after = jnp.maximum(before - primal_step * (cost - pull), 0.0)
                change = after - before
                square = square + change * change
                new_ref[here] = after
                message[here] = 2.0 * after - before
                if last and chunk == 0:
                    rest[0][:, lanes] = after
            squares.append(square)
        message[2 * sub] = squares[0] + squares[1]

    inputs = [own, other, *starts, weight]
    outputs = [(2 * sub, scen, tile), (2 * sub + 1, scen, tile)]
    if not first:
        inputs += [primal, primal_square]
        outputs.append((scen, tile))
    if last:
        outputs.append((scen, sub * tile))
    return call_once(body, inputs, outputs)


def dual_update(own, other, duals, weight, sub, last):
    _, scen, tile = own.shape

    def body(*refs):
        own_ref, other_ref, weight_ref = refs[:3]
        dual_refs = refs[3 : 3 + len(duals)]
        message, square_ref = refs[3 + len(duals) :][:2]
        square_ref[...] = own_ref[2 * sub] + other_ref[2 * sub]
        dual_step = step_scale * weight_ref[...]
        squares = []
        for chunk in range(2):
            square = jnp.zeros((scen, tile), F32)
            for k in range(sub):
                here = chunk * sub + k
                excess = own_ref[here] + other_ref[(1 - chunk) * sub + k]
                if len(duals) == 2:
                    before = unit_of(dual_refs[chunk], k, tile)
                else:
                    before = dual_refs[0][here]
                after = before - dual_step * excess
                change = after - before
                square = square + change * change
                if not last:
                    message[here] = after
                elif chunk == 0:
                    message[:, k * tile : (k + 1) * tile] = after
            squares.append(square)
        square = squares[0] + squares[1]
        if last:
            refs[-1][...] = square
        else:
            message[2 * sub] = square

    if last:
        outputs = [(scen, sub * tile), (scen, tile), (scen, tile)]
    else:
        outputs = [(2 * sub + 1, scen, tile), (scen, tile)]
    return call_once(body, [own, other, weight, *duals], outputs)


def summed(own, axis, others):
    got = [exchanged(value, axis, mask) for mask, value in enumerate(others, 1)]
    return (own + got[0]) + (got[1] + got[2])


def on_device(
    demand, lead_periods, matrix_tiles, tile_pos, cost_vector, primal_init, dual_init, weight_init
):
    band_bits = bit_count(lax.axis_size("band"))
    assert bit_count(lax.axis_size("col")) == 2 and band_bits >= 3
    matrix_tiles = matrix_tiles.reshape(matrix_tiles.shape[2:])
    positions = tile_pos.reshape(-1)
    tile = matrix_tiles.shape[-1]
    block_rows, scen = demand.shape
    sub = block_rows // tile
    units_col = sub << band_bits
    units_row = 4 * sub
    order = tuple(range(2, band_bits))

    row_unit, column_unit = positions // units_col, positions % units_col
    apart = (row_unit // sub) ^ lax.axis_index("col")
    row_place = ((apart & 1) * 2 + (apart >> 1)) * sub + row_unit % sub
    apart = (column_unit // sub) ^ lax.axis_index("band")
    column_place = (
        (apart & 3) * (units_col // 4) + bit_position(apart, order) * sub + column_unit % sub
    )
    index = jnp.concatenate([row_place, column_place])

    with jax.named_scope("dual_x"):
        dual_own = dual_init.T
        dual_beside = exchanged(dual_own, "col", 2)
        duals = [dual_own, dual_beside]
        parts = duals + [exchanged(value, "col", 1) for value in duals]
    demand_rows = demand.T
    earlier = []
    for steps in range(1, LEAD_MAX + 1):
        with jax.named_scope(f"lag_{steps}"):
            earlier.append(passed_along(demand_rows, "band", steps))
    right_side = right_side_of(demand_rows, earlier, lead_periods.reshape(sub, tile), tile)
    with jax.named_scope("start"):
        start_own = jnp.concatenate([primal_init.T, cost_vector[None, :]])
        starts = [start_own, exchanged(start_own, "band", 1 << order[-1])]
    weight = jnp.broadcast_to(weight_init[:, None], (scen, tile))
    primal = None
    primal_square = None
    for iteration in range(ITERS):
        last = iteration == ITERS - 1
        with jax.named_scope(f"back_{iteration}"):
            pieces = backward_product(index, parts, matrix_tiles, units_row, units_col, sub)
        total = summed(pieces[0], "band", pieces[1:])
        for bit in order[:-1]:
            half = total.shape[0] // 2
            send = jnp.concatenate([total[half:-1], total[-1:]])
            total = jnp.concatenate([total[:half], total[-1:]]) + exchanged(send, "band", 1 << bit)
        with jax.named_scope(f"pair_{iteration}"):
            other = exchanged(total, "band", 1 << order[-1])
        results = primal_update(total, other, starts, primal, weight, primal_square, sub, last)
        primal, ahead = results[:2]
        if iteration:
            weight = results[2]
        if last:
            primal_rows = results[-1]
        for bit in order[-2::-1]:
            got = exchanged(ahead, "band", 1 << bit)
            ahead = jnp.concatenate([ahead[:-1], got[:-1], ahead[-1:] + got[-1:]])
        with jax.named_scope(f"spread_{iteration}"):
            ahead = [ahead] + [exchanged(ahead, "band", mask) for mask in range(1, 4)]
        with jax.named_scope(f"fore_{iteration}"):
            keep, send = forward_product(
                index, ahead, matrix_tiles, right_side, units_row, units_col, sub
            )
        total = keep + exchanged(send, "col", 1)
        results = dual_update(total, exchanged(total, "col", 2), duals, weight, sub, last)
        primal_square = results[1]
        if last:
            dual_rows, _, square = results
        else:
            duals = [results[0]]
            parts = [results[0], exchanged(results[0], "col", 1)]
    square = square + exchanged(square, "col", 1)
    square = summed(square, "band", [square] * 3)
    for bit in order:
        square = square + exchanged(square, "band", 1 << bit)
    weight = next_weight(weight, primal_square, square)[:, 0]
    return (primal_rows.T, dual_rows.T, weight)


def solution(mesh):
    in_specs = (
        P(("band", "col"), None),
        P(("band", "col")),
        P("band", "col", None, None, None),
        P("band", "col", None),
        P(("band", "col")),
        P(("band", "col"), None),
        P(("band", "col"), None),
        P(),
    )
    out_specs = (P(("band", "col"), None), P(("band", "col"), None), P())
    return jax.shard_map(
        on_device, mesh=mesh, in_specs=in_specs, out_specs=out_specs, check_vma=False
    )
```

```python
import jax
import jax.numpy as jnp
from jax import lax
from jax.experimental import pallas as pl
from jax.experimental.pallas import tpu as pltpu
from jax.sharding import PartitionSpec as P

ITERS = 3
LEAD_MAX = 4
GROUP = 32
PIECE = 8
KERNEL_VMEM = 24 << 20

step_scale = 0.45
return_share = 0.6
epsilon = 1e-06
F32 = jnp.float32
BF16 = jnp.bfloat16


def bit_count(count):
    bits = count.bit_length() - 1
    assert count == 1 << bits and bits >= 2
    return bits


def bit_position(relative, order):
    bits = len(order)
    place = 0
    for step, bit in enumerate(order):
        place = place + (((relative >> bit) & 1) << (bits - 1 - step))
    return place


def exchanged(value, axis, mask):
    count = lax.axis_size(axis)
    return lax.ppermute(value, axis, [(source, source ^ mask) for source in range(count)])


def passed_along(value, axis, steps):
    count = lax.axis_size(axis)
    return lax.ppermute(value, axis, [(source, (source + steps) % count) for source in range(count)])


def halves(value):
    high = value.astype(BF16)
    low = (value - high.astype(F32)).astype(BF16)
    return high, low


def stacked(value):
    high, low = halves(value)
    return jnp.concatenate(
        [jnp.concatenate([high, high], 1), jnp.concatenate([low, low], 1)], 0
    )


def in_vmem(array):
    return pltpu.with_memory_space_constraint(array, pltpu.VMEM)


def call_in_vmem(body, inputs, outputs, scratch=(), index=None):
    spec = pl.BlockSpec(memory_space=pltpu.VMEM)
    first = [] if index is None else [index]
    return pl.pallas_call(
        body,
        out_shape=[pltpu.VMEM(shape, F32) for shape in outputs],
        in_specs=[pl.BlockSpec(memory_space=pltpu.SMEM)] * len(first) + [spec] * len(inputs),
        out_specs=[spec] * len(outputs),
        scratch_shapes=list(scratch),
        compiler_params=pltpu.CompilerParams(vmem_limit_bytes=KERNEL_VMEM),
    )(*first, *(in_vmem(array) for array in inputs))


def unit_of(ref, k, tile):
    return ref[:, k * tile : (k + 1) * tile] if len(ref.shape) == 2 else ref[k]


def prepared_tiles(matrix_tiles):
    count, tile, _ = matrix_tiles.shape
    piece = min(PIECE, count)
    pieces = count // piece

    def body(tiles_ref, plain_ref, turned_ref, held, arrived):
        def copy_of(which):
            return pltpu.make_async_copy(
                tiles_ref.at[pl.ds(which * piece, piece)],
                held.at[pl.ds(which * piece, piece)],
                arrived.at[which],
            )

        for which in range(pieces):
            copy_of(which).start()

        def one_piece(which, carry):
            copy_of(which).wait()
            for k in range(piece):
                t = which * piece + k
                high, low = halves(held[t])
                plain_ref[t, :tile] = high
                plain_ref[t, tile:] = low
                turned_ref[t, :tile] = high.T
                turned_ref[t, tile:] = low.T
            return carry

        lax.fori_loop(0, pieces, one_piece, 0)

    spec = pl.BlockSpec(memory_space=pltpu.VMEM)
    return pl.pallas_call(
        body,
        out_shape=[pltpu.VMEM((count, 2 * tile, tile), BF16)] * 2,
        in_specs=[pl.BlockSpec(memory_space=pl.ANY)],
        out_specs=[spec] * 2,
        scratch_shapes=[
            pltpu.VMEM((count, tile, tile), F32),
            pltpu.SemaphoreType.DMA((pieces,)),
        ],
        compiler_params=pltpu.CompilerParams(vmem_limit_bytes=KERNEL_VMEM),
    )(matrix_tiles)


def tile_products(index, parts, tiles, from_row, operand_units, total_units, finish, extra, outputs):
    count, _, tile = tiles.shape
    scen = parts[0].shape[-2]
    group = min(GROUP, count)
    given = len(parts) + len(extra)

    def body(index_ref, tiles_ref, *refs):
        part_refs = refs[: len(parts)]
        extra_refs = refs[len(parts) : given]
        out_refs = refs[given:-2]
        total, operand = refs[-2:]
        total[...] = jnp.zeros_like(total)
        per_part = operand_units // len(parts)
        for which, ref in enumerate(part_refs):
            for k in range(per_part):
                operand[which * per_part + k] = stacked(unit_of(ref, k, tile))

        def one_group(step, carry):
            for k in range(group):
                t = step * group + k
                row = index_ref[t]
                column = index_ref[count + t]
                source, target = (row, column) if from_row else (column, row)
                product = jnp.dot(operand[source], tiles_ref[t], preferred_element_type=F32)
                total[target] += product[:scen] + product[scen:]
            return carry

        lax.fori_loop(0, count // group, one_group, 0)
        finish(part_refs, extra_refs, total, out_refs)

    return call_in_vmem(
        body,
        [tiles, *parts, *extra],
        outputs,
        [
            pltpu.VMEM((total_units, scen, tile), F32),
            pltpu.VMEM((operand_units, 2 * scen, 2 * tile), BF16),
        ],
        index,
    )


def backward_product(index, parts, tiles, units_row, units_col):
    scen, tile = parts[0].shape[-2], tiles.shape[-1]
    quarter = units_col // 4
    carried = len(parts) == 2

    def finish(part_refs, extra_refs, total, out_refs):
        for mask in range(4):
            for k in range(quarter):
                out_refs[mask][k] = total[mask * quarter + k]
        if carried:
            square = part_refs[0][units_row // 2] + part_refs[1][units_row // 2]
        else:
            square = jnp.zeros((scen, tile), F32)
        for mask in range(4):
            out_refs[mask][quarter] = square

    return tile_products(
        index, parts, tiles, True, units_row, units_col, finish, [],
        [(quarter + 1, scen, tile)] * 4,
    )


def forward_product(index, parts, tiles, right_side, units_row, units_col, sub):
    _, scen, tile = parts[0].shape
    quarter = units_col // 4
    half = units_row // 2

    def finish(part_refs, extra_refs, total, out_refs):
        keep, send = out_refs
        for k in range(half):
            value = total[k]
            keep[k] = value - extra_refs[0][k] if k < sub else value
            send[k] = total[half + k]
        squares = [ref[quarter] for ref in part_refs]
        square = (squares[0] + squares[1]) + (squares[2] + squares[3])
        keep[half] = square
        send[half] = square

    return tile_products(
        index, parts, tiles, False, units_col, units_row, finish, [right_side],
        [(half + 1, scen, tile)] * 2,
    )


def right_side_of(demand_rows, earlier, lead, tile):
    scen, rows = demand_rows.shape
    sub = rows // tile

    def body(demand_ref, *refs):
        lead_ref, out_ref = refs[-2:]
        for k in range(sub):
            lanes = slice(k * tile, (k + 1) * tile)
            wanted = lead_ref[k : k + 1, :]
            lagged = jnp.zeros((scen, tile), F32)
            for steps in range(1, LEAD_MAX + 1):
                lagged = jnp.where(wanted == steps, refs[steps - 1][:, lanes], lagged)
            out_ref[k] = demand_ref[:, lanes] - return_share * lagged

    return call_in_vmem(body, (demand_rows, *earlier, lead), ((sub, scen, tile),))[0]


def next_weight(weight, primal_square, dual_square):
    primal_sum = jnp.sum(primal_square, axis=-1, keepdims=True)
    dual_sum = jnp.sum(dual_square, axis=-1, keepdims=True)
    ratio = (primal_sum + epsilon) / (dual_sum + epsilon)
    return jnp.sqrt(weight * jnp.sqrt(ratio))


def primal_update(own, other, starts, primal, weight, primal_square, sub, last):
    _, scen, tile = own.shape
    first = primal is None

    def body(*refs):
        own_ref, other_ref = refs[:2]
        start_refs = refs[2:4]
        weight_ref = refs[4]
        rest = refs[5:]
        if not first:
            primal_ref, square_ref = rest[:2]
            rest = rest[2:]
        new_ref, message = rest[:2]
        rest = rest[2:]
        weight_now = weight_ref[...]
        if not first:
            weight_now = next_weight(
                weight_now, square_ref[...], own_ref[2 * sub] + other_ref[2 * sub]
            )
            rest[0][...] = weight_now
            rest = rest[1:]
        primal_step = step_scale / weight_now
        squares = []
        for chunk in range(2):
            square = jnp.zeros((scen, tile), F32)
            for k in range(sub):
                here = chunk * sub + k
                lanes = slice(k * tile, (k + 1) * tile)
                pull = own_ref[here] + other_ref[(1 - chunk) * sub + k]
                before = start_refs[chunk][:scen, lanes] if first else primal_ref[here]
                cost = start_refs[chunk][scen : scen + 1, lanes]
                after = jnp.maximum(before - primal_step * (cost - pull), 0.0)
                change = after - before
                square = square + change * change
                new_ref[here] = after
                message[here] = 2.0 * after - before
                if last and chunk == 0:
                    rest[0][:, lanes] = after
            squares.append(square)
        message[2 * sub] = squares[0] + squares[1]

    inputs = [own, other, *starts, weight]
    outputs = [(2 * sub, scen, tile), (2 * sub + 1, scen, tile)]
    if not first:
        inputs += [primal, primal_square]
        outputs.append((scen, tile))
    if last:
        outputs.append((scen, sub * tile))
    return call_in_vmem(body, inputs, outputs)


def dual_update(own, other, duals, weight, sub, last):
    _, scen, tile = own.shape

    def body(*refs):
        own_ref, other_ref, weight_ref = refs[:3]
        dual_refs = refs[3 : 3 + len(duals)]
        message, square_ref = refs[3 + len(duals) :][:2]
        square_ref[...] = own_ref[2 * sub] + other_ref[2 * sub]
        dual_step = step_scale * weight_ref[...]
        squares = []
        for chunk in range(2):
            square = jnp.zeros((scen, tile), F32)
            for k in range(sub):
                here = chunk * sub + k
                excess = own_ref[here] + other_ref[(1 - chunk) * sub + k]
                if len(duals) == 2:
                    before = unit_of(dual_refs[chunk], k, tile)
                else:
                    before = dual_refs[0][here]
                after = before - dual_step * excess
                change = after - before
                square = square + change * change
                if not last:
                    message[here] = after
                elif chunk == 0:
                    message[:, k * tile : (k + 1) * tile] = after
            squares.append(square)
        square = squares[0] + squares[1]
        if last:
            refs[-1][...] = square
        else:
            message[2 * sub] = square

    if last:
        outputs = [(scen, sub * tile), (scen, tile), (scen, tile)]
    else:
        outputs = [(2 * sub + 1, scen, tile), (scen, tile)]
    return call_in_vmem(body, [own, other, weight, *duals], outputs)


def summed(own, axis, others):
    got = [exchanged(value, axis, mask) for mask, value in enumerate(others, 1)]
    return (own + got[0]) + (got[1] + got[2])


def on_device(
    demand, lead_periods, matrix_tiles, tile_pos, cost_vector, primal_init, dual_init, weight_init
):
    band_bits = bit_count(lax.axis_size("band"))
    assert bit_count(lax.axis_size("col")) == 2 and band_bits >= 3
    matrix_tiles = matrix_tiles.reshape(matrix_tiles.shape[2:])
    positions = tile_pos.reshape(-1)
    tile = matrix_tiles.shape[-1]
    block_rows, scen = demand.shape
    sub = block_rows // tile
    units_col = sub << band_bits
    units_row = 4 * sub
    order = tuple(range(2, band_bits))

    row_unit, column_unit = positions // units_col, positions % units_col
    apart = (row_unit // sub) ^ lax.axis_index("col")
    row_place = ((apart & 1) * 2 + (apart >> 1)) * sub + row_unit % sub
    apart = (column_unit // sub) ^ lax.axis_index("band")
    column_place = (
        (apart & 3) * (units_col // 4) + bit_position(apart, order) * sub + column_unit % sub
    )
    index = jnp.concatenate([row_place, column_place])

    with jax.named_scope("dual_x"):
        dual_own = dual_init.T
        dual_beside = exchanged(dual_own, "col", 2)
        duals = [dual_own, dual_beside]
        parts = duals + [exchanged(value, "col", 1) for value in duals]
    with jax.named_scope("tiles"):
        plain_tiles, turned_tiles = prepared_tiles(matrix_tiles)
    demand_rows = demand.T
    earlier = []
    for steps in range(1, LEAD_MAX + 1):
        with jax.named_scope(f"lag_{steps}"):
            earlier.append(passed_along(demand_rows, "band", steps))
    right_side = right_side_of(demand_rows, earlier, lead_periods.reshape(sub, tile), tile)
    with jax.named_scope("start"):
        start_own = jnp.concatenate([primal_init.T, cost_vector[None, :]])
        starts = [start_own, exchanged(start_own, "band", 1 << order[-1])]
    weight = jnp.broadcast_to(weight_init[:, None], (scen, tile))
    primal = None
    primal_square = None
    for iteration in range(ITERS):
        last = iteration == ITERS - 1
        with jax.named_scope(f"back_{iteration}"):
            pieces = backward_product(index, parts, plain_tiles, units_row, units_col)
        total = summed(pieces[0], "band", pieces[1:])
        for bit in order[:-1]:
            half = total.shape[0] // 2
            send = jnp.concatenate([total[half:-1], total[-1:]])
            total = jnp.concatenate([total[:half], total[-1:]]) + exchanged(send, "band", 1 << bit)
        with jax.named_scope(f"pair_{iteration}"):
            other = exchanged(total, "band", 1 << order[-1])
        results = primal_update(total, other, starts, primal, weight, primal_square, sub, last)
        primal, ahead = results[:2]
        if iteration:
            weight = results[2]
        if last:
            primal_rows = results[-1]
        for bit in order[-2::-1]:
            got = exchanged(ahead, "band", 1 << bit)
            ahead = jnp.concatenate([ahead[:-1], got[:-1], ahead[-1:] + got[-1:]])
        with jax.named_scope(f"spread_{iteration}"):
            ahead = [ahead] + [exchanged(ahead, "band", mask) for mask in range(1, 4)]
        with jax.named_scope(f"fore_{iteration}"):
            keep, send = forward_product(
                index, ahead, turned_tiles, right_side, units_row, units_col, sub
            )
        total = keep + exchanged(send, "col", 1)
        results = dual_update(total, exchanged(total, "col", 2), duals, weight, sub, last)
        primal_square = results[1]
        if last:
            dual_rows, _, square = results
        else:
            duals = [results[0]]
            parts = [results[0], exchanged(results[0], "col", 1)]
    square = square + exchanged(square, "col", 1)
    square = summed(square, "band", [square] * 3)
    for bit in order:
        square = square + exchanged(square, "band", 1 << bit)
    weight = next_weight(weight, primal_square, square)[:, 0]
    return (primal_rows.T, dual_rows.T, weight)


def solution(mesh):
    in_specs = (
        P(("band", "col"), None),
        P(("band", "col")),
        P("band", "col", None, None, None),
        P("band", "col", None),
        P(("band", "col")),
        P(("band", "col"), None),
        P(("band", "col"), None),
        P(),
    )
    out_specs = (P(("band", "col"), None), P(("band", "col"), None), P())
    return jax.shard_map(
        on_device, mesh=mesh, in_specs=in_specs, out_specs=out_specs, check_vma=False
    )
```

```python
import math

import jax
import jax.numpy as jnp
from jax import lax
from jax.experimental import pallas as pl
from jax.experimental.pallas import tpu as pltpu
from jax.sharding import PartitionSpec as P


ITERS = 3
LEAD_MAX = 4
GROUP = 32
PIECE = 8
STREAMS = 2
KERNEL_VMEM = 1 << 20

step_scale = 0.45
return_share = 0.6
epsilon = 1e-06
F32 = jnp.float32
BF16 = jnp.bfloat16


def bit_count(count):
    bits = count.bit_length() - 1
    assert count == 1 << bits and bits >= 2
    return bits


def bit_position(relative, order):
    bits = len(order)
    place = 0
    for step, bit in enumerate(order):
        place = place + (((relative >> bit) & 1) << (bits - 1 - step))
    return place


def exchanged(value, axis, mask):
    count = lax.axis_size(axis)
    return lax.ppermute(value, axis, [(source, source ^ mask) for source in range(count)])


def passed_along(value, axis, steps):
    count = lax.axis_size(axis)
    return lax.ppermute(value, axis, [(source, (source + steps) % count) for source in range(count)])


def halves(value):
    high = value.astype(BF16)
    low = (value - high.astype(F32)).astype(BF16)
    return high, low


def stacked(value):
    high, low = halves(value)
    return jnp.concatenate(
        [jnp.concatenate([high, high], 1), jnp.concatenate([low, low], 1)], 0
    )


def in_vmem(array):
    return pltpu.with_memory_space_constraint(array, pltpu.VMEM)


def call_in_vmem(body, inputs, outputs, scratch=(), index=None):
    spec = pl.BlockSpec(memory_space=pltpu.VMEM)
    first = [] if index is None else [index]
    room = KERNEL_VMEM + sum(math.prod(ref.shape) * ref.dtype.itemsize for ref in scratch)
    return pl.pallas_call(
        body,
        out_shape=[pltpu.VMEM(shape, F32) for shape in outputs],
        in_specs=[pl.BlockSpec(memory_space=pltpu.SMEM)] * len(first) + [spec] * len(inputs),
        out_specs=[spec] * len(outputs),
        scratch_shapes=list(scratch),
        compiler_params=pltpu.CompilerParams(vmem_limit_bytes=room),
    )(*first, *(in_vmem(array) for array in inputs))


def unit_of(ref, k, tile, rows):
    return ref[rows, k * tile : (k + 1) * tile] if len(ref.shape) == 2 else ref[k]


def prepared(matrix_tiles, primal_rows, cost_row):
    count, tile, _ = matrix_tiles.shape
    scen, rows = primal_rows.shape
    piece = min(PIECE, count)
    pieces = count // piece

    def body(tiles_ref, primal_ref, cost_ref, plain_ref, turned_ref, start_ref, held, arrived, small):
        def copy_of(which):
            return pltpu.make_async_copy(
                tiles_ref.at[pl.ds(which * piece, piece)],
                held.at[pl.ds(which * piece, piece)],
                arrived.at[which],
            )

        copy_primal = pltpu.make_async_copy(primal_ref, start_ref.at[pl.ds(0, scen)], small.at[0])
        copy_cost = pltpu.make_async_copy(cost_ref, start_ref.at[pl.ds(scen, 1)], small.at[1])
        for which in range(pieces):
            copy_of(which).start()
        copy_primal.start()
        copy_cost.start()

        def one_piece(which, carry):
            copy_of(which).wait()
            for k in range(piece):
                t = which * piece + k
                high, low = halves(held[t])
                plain_ref[t, :tile] = high
                plain_ref[t, tile:] = low
                turned_ref[t, :tile] = high.T
                turned_ref[t, tile:] = low.T
            return carry

        lax.fori_loop(0, pieces, one_piece, 0)
        copy_primal.wait()
        copy_cost.wait()

    anywhere = pl.BlockSpec(memory_space=pl.ANY)
    spec = pl.BlockSpec(memory_space=pltpu.VMEM)
    in_hbm = [
        pltpu.with_memory_space_constraint(array, pltpu.HBM)
        for array in (matrix_tiles, primal_rows, cost_row)
    ]
    return pl.pallas_call(
        body,
        out_shape=[
            pltpu.VMEM((count, 2 * tile, tile), BF16),
            pltpu.VMEM((count, 2 * tile, tile), BF16),
            pltpu.VMEM((scen + 1, rows), F32),
        ],
        in_specs=[anywhere] * 3,
        out_specs=[spec] * 3,
        scratch_shapes=[
            pltpu.VMEM((count, tile, tile), F32),
            pltpu.SemaphoreType.DMA((pieces,)),
            pltpu.SemaphoreType.DMA((2,)),
        ],
        compiler_params=pltpu.CompilerParams(
            vmem_limit_bytes=KERNEL_VMEM + count * tile * tile * 4
        ),
    )(*in_hbm)


def tile_products(index, parts, tiles, rows, from_row, operand_units, total_units, finish, extra, outputs):
    count, _, tile = tiles.shape
    scen = rows.stop - rows.start
    group = min(GROUP, count)
    given = len(parts) + len(extra)

    def body(index_ref, tiles_ref, *refs):
        part_refs = refs[: len(parts)]
        extra_refs = refs[len(parts) : given]
        out_refs = refs[given:-2]
        total, operand = refs[-2:]
        total[...] = jnp.zeros_like(total)
        per_part = operand_units // len(parts)
        for which, ref in enumerate(part_refs):
            for k in range(per_part):
                operand[which * per_part + k] = stacked(unit_of(ref, k, tile, rows))

        def one_group(step, carry):
            for k in range(group):
                t = step * group + k
                row = index_ref[t]
                column = index_ref[count + t]
                source, target = (row, column) if from_row else (column, row)
                product = jnp.dot(operand[source], tiles_ref[t], preferred_element_type=F32)
                total[target] += product[:scen] + product[scen:]
            return carry

        lax.fori_loop(0, count // group, one_group, 0)
        finish(part_refs, extra_refs, total, out_refs)

    return call_in_vmem(
        body,
        [tiles, *parts, *extra],
        outputs,
        [
            pltpu.VMEM((total_units, scen, tile), F32),
            pltpu.VMEM((operand_units, 2 * scen, 2 * tile), BF16),
        ],
        index,
    )


def backward_product(index, parts, tiles, rows, units_row, units_col):
    scen, tile = rows.stop - rows.start, tiles.shape[-1]
    quarter = units_col // 4
    carried = len(parts) == 2

    def finish(part_refs, extra_refs, total, out_refs):
        for mask in range(4):
            for k in range(quarter):
                out_refs[mask][k] = total[mask * quarter + k]
        if carried:
            square = part_refs[0][units_row // 2] + part_refs[1][units_row // 2]
        else:
            square = jnp.zeros((scen, tile), F32)
        for mask in range(4):
            out_refs[mask][quarter] = square

    return tile_products(
        index, parts, tiles, rows, True, units_row, units_col, finish, [],
        [(quarter + 1, scen, tile)] * 4,
    )


def forward_product(index, parts, tiles, rows, units_row, units_col):
    _, scen, tile = parts[0].shape
    quarter = units_col // 4
    half = units_row // 2

    def finish(part_refs, extra_refs, total, out_refs):
        keep, send = out_refs
        for k in range(half):
            keep[k] = total[k]
            send[k] = total[half + k]
        squares = [ref[quarter] for ref in part_refs]
        square = (squares[0] + squares[1]) + (squares[2] + squares[3])
        keep[half] = square
        send[half] = square

    return tile_products(
        index, parts, tiles, rows, False, units_col, units_row, finish, [],
        [(half + 1, scen, tile)] * 2,
    )


def right_sides_of(demand_rows, earlier, lead, tile, share):
    scen, rows = demand_rows.shape
    sub = rows // tile

    def body(demand_ref, *refs):
        earlier_refs, lead_ref, out_refs = refs[:LEAD_MAX], refs[LEAD_MAX], refs[LEAD_MAX + 1 :]
        for half, out_ref in enumerate(out_refs):
            own = slice(half * share, (half + 1) * share)
            for k in range(sub):
                lanes = slice(k * tile, (k + 1) * tile)
                wanted = lead_ref[k : k + 1, :]
                lagged = jnp.zeros((share, tile), F32)
                for steps in range(1, LEAD_MAX + 1):
                    lagged = jnp.where(wanted == steps, earlier_refs[steps - 1][own, lanes], lagged)
                out_ref[k] = demand_ref[own, lanes] - return_share * lagged
            for k in range(sub, 2 * sub + 1):
                out_ref[k] = jnp.zeros((share, tile), F32)

    return call_in_vmem(
        body,
        (demand_rows, *earlier, lead),
        [(2 * sub + 1, share, tile)] * (scen // share),
    )


def next_weight(weight, primal_square, dual_square):
    primal_sum = jnp.sum(primal_square, axis=-1, keepdims=True)
    dual_sum = jnp.sum(dual_square, axis=-1, keepdims=True)
    ratio = (primal_sum + epsilon) / (dual_sum + epsilon)
    return jnp.sqrt(weight * jnp.sqrt(ratio))


def primal_update(own, other, starts, primal, weight, primal_square, rows, sub, last):
    _, scen, tile = own.shape
    all_scen = starts[0].shape[0] - 1
    first = primal is None

    def body(*refs):
        own_ref, other_ref = refs[:2]
        start_refs = refs[2:4]
        weight_ref = refs[4]
        rest = refs[5:]
        if not first:
            primal_ref, square_ref = rest[:2]
            rest = rest[2:]
        new_ref, message = rest[:2]
        rest = rest[2:]
        weight_now = weight_ref[...]
        if not first:
            weight_now = next_weight(
                weight_now, square_ref[...], own_ref[2 * sub] + other_ref[2 * sub]
            )
            rest[0][...] = weight_now
            rest = rest[1:]
        primal_step = step_scale / weight_now
        squares = []
        for chunk in range(2):
            square = jnp.zeros((scen, tile), F32)
            for k in range(sub):
                here = chunk * sub + k
                lanes = slice(k * tile, (k + 1) * tile)
                pull = own_ref[here] + other_ref[(1 - chunk) * sub + k]
                before = start_refs[chunk][rows, lanes] if first else primal_ref[here]
                cost = start_refs[chunk][all_scen : all_scen + 1, lanes]
                after = jnp.maximum(before - primal_step * (cost - pull), 0.0)
                change = after - before
                square = square + change * change
                new_ref[here] = after
                message[here] = 2.0 * after - before
                if last and chunk == 0:
                    rest[0][:, lanes] = after
            squares.append(square)
        message[2 * sub] = squares[0] + squares[1]

    inputs = [own, other, *starts, weight]
    outputs = [(2 * sub, scen, tile), (2 * sub + 1, scen, tile)]
    if not first:
        inputs += [primal, primal_square]
        outputs.append((scen, tile))
    if last:
        outputs.append((scen, sub * tile))
    return call_in_vmem(body, inputs, outputs)


def dual_update(own, other, duals, weight, rows, sub, last):
    _, scen, tile = own.shape

    def body(*refs):
        own_ref, other_ref, weight_ref = refs[:3]
        dual_refs = refs[3 : 3 + len(duals)]
        message, square_ref = refs[3 + len(duals) :][:2]
        square_ref[...] = own_ref[2 * sub] + other_ref[2 * sub]
        dual_step = step_scale * weight_ref[...]
        squares = []
        for chunk in range(2):
            square = jnp.zeros((scen, tile), F32)
            for k in range(sub):
                here = chunk * sub + k
                excess = own_ref[here] + other_ref[(1 - chunk) * sub + k]
                if len(duals) == 2:
                    before = unit_of(dual_refs[chunk], k, tile, rows)
                else:
                    before = dual_refs[0][here]
                after = before - dual_step * excess
                change = after - before
                square = square + change * change
                if not last:
                    message[here] = after
                elif chunk == 0:
                    message[:, k * tile : (k + 1) * tile] = after
            squares.append(square)
        square = squares[0] + squares[1]
        if last:
            refs[-1][...] = square
        else:
            message[2 * sub] = square

    if last:
        outputs = [(scen, sub * tile), (scen, tile), (scen, tile)]
    else:
        outputs = [(2 * sub + 1, scen, tile), (scen, tile)]
    return call_in_vmem(body, [own, other, weight, *duals], outputs)


def summed(own, axis, others):
    got = [exchanged(value, axis, mask) for mask, value in enumerate(others, 1)]
    return (own + got[0]) + (got[1] + got[2])


def every_step(
    demand, lead_periods, matrix_tiles, tile_pos, cost_vector, primal_init, dual_init, weight_init
):
    band_bits = bit_count(lax.axis_size("band"))
    assert bit_count(lax.axis_size("col")) == 2 and band_bits >= 3
    matrix_tiles = matrix_tiles.reshape(matrix_tiles.shape[2:])
    positions = tile_pos.reshape(-1)
    tile = matrix_tiles.shape[-1]
    block_rows, scen = demand.shape
    sub = block_rows // tile
    units_col = sub << band_bits
    units_row = 4 * sub
    order = tuple(range(2, band_bits))

    row_unit, column_unit = positions // units_col, positions % units_col
    apart = (row_unit // sub) ^ lax.axis_index("col")
    row_place = ((apart & 1) * 2 + (apart >> 1)) * sub + row_unit % sub
    apart = (column_unit // sub) ^ lax.axis_index("band")
    column_place = (
        (apart & 3) * (units_col // 4) + bit_position(apart, order) * sub + column_unit % sub
    )
    index = jnp.concatenate([row_place, column_place])

    demand_rows, dual_rows, primal_rows = demand.T, dual_init.T, primal_init.T
    dual_pair = [dual_rows, exchanged(dual_rows, "col", 2)]
    earlier = []
    for steps in range(1, LEAD_MAX + 1):
        earlier.append(passed_along(demand_rows, "band", steps))
    plain_tiles, turned_tiles, start_rows = prepared(
        matrix_tiles, primal_rows, cost_vector[None, :]
    )
    dual_pair += [exchanged(value, "col", 1) for value in dual_pair]
    start_rows = [start_rows, exchanged(start_rows, "band", 1 << order[-1])]
    share = scen // STREAMS
    right_sides = right_sides_of(demand_rows, earlier, lead_periods.reshape(sub, tile), tile, share)
    states = []
    for stream in range(STREAMS):
        rows = slice(stream * share, (stream + 1) * share)
        states.append(
            dict(
                rows=rows,
                parts=dual_pair,
                duals=dual_pair[:2],
                weight=jnp.broadcast_to(weight_init[rows, None], (share, tile)),
                primal=None,
                primal_square=None,
                right_side=right_sides[stream],
            )
        )

    def step_of(state, iteration):
        last = iteration == ITERS - 1
        rows = state["rows"]
        pieces = backward_product(index, state["parts"], plain_tiles, rows, units_row, units_col)
        total = summed(pieces[0], "band", pieces[1:])
        for bit in order[:-1]:
            half = total.shape[0] // 2
            send = jnp.concatenate([total[half:-1], total[-1:]])
            total = jnp.concatenate([total[:half], total[-1:]]) + exchanged(send, "band", 1 << bit)
        other = exchanged(total, "band", 1 << order[-1])
        results = primal_update(
            total, other, start_rows, state["primal"], state["weight"],
            state["primal_square"], rows, sub, last,
        )
        state["primal"], ahead = results[:2]
        if iteration:
            state["weight"] = results[2]
        if last:
            state["primal_rows"] = results[-1]
        for bit in order[-2::-1]:
            got = exchanged(ahead, "band", 1 << bit)
            ahead = jnp.concatenate([ahead[:-1], got[:-1], ahead[-1:] + got[-1:]])
        ahead = [ahead] + [exchanged(ahead, "band", mask) for mask in range(1, 4)]
        keep, send = forward_product(index, ahead, turned_tiles, rows, units_row, units_col)
        total = (keep + exchanged(send, "col", 1)) - state["right_side"]
        other = exchanged(total, "col", 2)
        results = dual_update(total, other, state["duals"], state["weight"], rows, sub, last)
        state["primal_square"] = results[1]
        if last:
            state["dual_rows"], _, state["square"] = results
        else:
            state["duals"] = [results[0]]
            state["parts"] = [results[0], exchanged(results[0], "col", 1)]

    for iteration in range(ITERS):
        for state in states:
            step_of(state, iteration)

    def joined(name):
        return jnp.concatenate([state[name] for state in states])

    square = joined("square")
    square = square + exchanged(square, "col", 1)
    square = summed(square, "band", [square] * 3)
    for bit in order:
        square = square + exchanged(square, "band", 1 << bit)
    weight = next_weight(joined("weight"), joined("primal_square"), square)[:, 0]
    return (joined("primal_rows").T, joined("dual_rows").T, weight)


def solution(mesh):
    in_specs = (
        P(("band", "col"), None),
        P(("band", "col")),
        P("band", "col", None, None, None),
        P("band", "col", None),
        P(("band", "col")),
        P(("band", "col"), None),
        P(("band", "col"), None),
        P(),
    )
    out_specs = (P(("band", "col"), None), P(("band", "col"), None), P())
    return jax.shard_map(
        every_step, mesh=mesh, in_specs=in_specs, out_specs=out_specs, check_vma=False
    )
```

```python
import math

import jax
import jax.numpy as jnp
from jax import lax
from jax.experimental import pallas as pl
from jax.experimental.pallas import tpu as pltpu
from jax.sharding import PartitionSpec as P


ITERS = 3
LEAD_MAX = 4
GROUP = 128
PIECE = 8
AHEAD = 16
STREAMS = 2
KERNEL_VMEM = 1 << 20

step_scale = 0.45
return_share = 0.6
epsilon = 1e-06
F32 = jnp.float32
BF16 = jnp.bfloat16


def bit_count(count):
    bits = count.bit_length() - 1
    assert count == 1 << bits and bits >= 2
    return bits


def bit_position(relative, order):
    bits = len(order)
    place = 0
    for step, bit in enumerate(order):
        place = place + (((relative >> bit) & 1) << (bits - 1 - step))
    return place


def exchanged(value, axis, mask):
    count = lax.axis_size(axis)
    return lax.ppermute(value, axis, [(source, source ^ mask) for source in range(count)])


def passed_along(value, axis, steps):
    count = lax.axis_size(axis)
    return lax.ppermute(value, axis, [(source, (source + steps) % count) for source in range(count)])


def halves(value):
    high = value.astype(BF16)
    low = (value - high.astype(F32)).astype(BF16)
    return high, low


def stacked(value):
    high, low = halves(value)
    return jnp.concatenate(
        [jnp.concatenate([high, high], 1), jnp.concatenate([low, low], 1)], 0
    )


def in_vmem(array):
    return pltpu.with_memory_space_constraint(array, pltpu.VMEM)


def call_in_vmem(body, inputs, outputs, scratch=(), index=None):
    spec = pl.BlockSpec(memory_space=pltpu.VMEM)
    first = [] if index is None else [index]
    room = KERNEL_VMEM + sum(math.prod(ref.shape) * ref.dtype.itemsize for ref in scratch)
    return pl.pallas_call(
        body,
        out_shape=[pltpu.VMEM(shape, F32) for shape in outputs],
        in_specs=[pl.BlockSpec(memory_space=pltpu.SMEM)] * len(first) + [spec] * len(inputs),
        out_specs=[spec] * len(outputs),
        scratch_shapes=list(scratch),
        compiler_params=pltpu.CompilerParams(vmem_limit_bytes=room),
    )(*first, *(in_vmem(array) for array in inputs))


def unit_of(ref, k, tile, rows):
    return ref[rows, k * tile : (k + 1) * tile] if len(ref.shape) == 2 else ref[k]


def prepared(matrix_tiles, message_rows):
    count, tile, _ = matrix_tiles.shape
    heights = [array.shape[0] for array in message_rows]
    piece = min(PIECE, count)
    pieces = count // piece
    ahead = min(AHEAD, pieces)

    def body(tiles_ref, *refs):
        row_refs = refs[: len(heights)]
        plain_ref, turned_ref, start_ref, held, arrived, small = refs[len(heights) :]

        def copy_of(which):
            return pltpu.make_async_copy(
                tiles_ref.at[pl.ds(which * piece, piece)],
                held.at[pl.ds(which * piece, piece)],
                arrived.at[which],
            )

        row_copies = [
            pltpu.make_async_copy(
                ref, start_ref.at[pl.ds(sum(heights[:which]), heights[which])], small.at[which]
            )
            for which, ref in enumerate(row_refs)
        ]
        for which in range(ahead):
            copy_of(which).start()
        for copy in row_copies:
            copy.start()

        def one_piece(which, carry):
            @pl.when(which + ahead < pieces)
            def _():
                copy_of(which + ahead).start()

            copy_of(which).wait()
            for k in range(piece):
                t = which * piece + k
                high, low = halves(held[t])
                plain_ref[t, :tile] = high
                plain_ref[t, tile:] = low
                turned_ref[t, :tile] = high.T
                turned_ref[t, tile:] = low.T
            return carry

        lax.fori_loop(0, pieces, one_piece, 0)
        for copy in row_copies:
            copy.wait()

    anywhere = pl.BlockSpec(memory_space=pl.ANY)
    spec = pl.BlockSpec(memory_space=pltpu.VMEM)
    in_hbm = [
        pltpu.with_memory_space_constraint(array, pltpu.HBM)
        for array in (matrix_tiles, *message_rows)
    ]
    return pl.pallas_call(
        body,
        out_shape=[
            pltpu.VMEM((count, 2 * tile, tile), BF16),
            pltpu.VMEM((count, 2 * tile, tile), BF16),
            pltpu.VMEM((sum(heights), message_rows[0].shape[1]), F32),
        ],
        in_specs=[anywhere] * len(in_hbm),
        out_specs=[spec] * 3,
        scratch_shapes=[
            pltpu.VMEM((count, tile, tile), F32),
            pltpu.SemaphoreType.DMA((pieces,)),
            pltpu.SemaphoreType.DMA((len(heights),)),
        ],
        compiler_params=pltpu.CompilerParams(
            vmem_limit_bytes=KERNEL_VMEM + count * tile * tile * 4
        ),
    )(*in_hbm)


def tile_products(index, parts, tiles, rows, from_row, operand_units, total_units, finish, extra, outputs):
    count, _, tile = tiles.shape
    scen = rows.stop - rows.start
    group = min(GROUP, count)
    given = len(parts) + len(extra)

    def body(index_ref, tiles_ref, *refs):
        part_refs = refs[: len(parts)]
        extra_refs = refs[len(parts) : given]
        out_refs = refs[given:-2]
        total, operand = refs[-2:]
        total[...] = jnp.zeros_like(total)
        per_part = operand_units // len(parts)
        for which, ref in enumerate(part_refs):
            for k in range(per_part):
                operand[which * per_part + k] = stacked(unit_of(ref, k, tile, rows))

        def one_group(step, carry):
            for k in range(group):
                t = step * group + k
                row = index_ref[t]
                column = index_ref[count + t]
                source, target = (row, column) if from_row else (column, row)
                product = jnp.dot(operand[source], tiles_ref[t], preferred_element_type=F32)
                total[target] += product[:scen] + product[scen:]
            return carry

        lax.fori_loop(0, count // group, one_group, 0)
        finish(part_refs, extra_refs, total, out_refs)

    return call_in_vmem(
        body,
        [tiles, *parts, *extra],
        outputs,
        [
            pltpu.VMEM((total_units, scen, tile), F32),
            pltpu.VMEM((operand_units, 2 * scen, 2 * tile), BF16),
        ],
        index,
    )


def backward_product(index, parts, tiles, rows, units_row, units_col):
    scen, tile = rows.stop - rows.start, tiles.shape[-1]
    quarter = units_col // 4
    carried = len(parts) == 2

    def finish(part_refs, extra_refs, total, out_refs):
        for mask in range(4):
            for k in range(quarter):
                out_refs[mask][k] = total[mask * quarter + k]
        if carried:
            square = part_refs[0][units_row // 2] + part_refs[1][units_row // 2]
        else:
            square = jnp.zeros((scen, tile), F32)
        for mask in range(4):
            out_refs[mask][quarter] = square

    return tile_products(
        index, parts, tiles, rows, True, units_row, units_col, finish, [],
        [(quarter + 1, scen, tile)] * 4,
    )


def forward_product(index, parts, tiles, rows, units_row, units_col):
    _, scen, tile = parts[0].shape
    quarter = units_col // 4
    half = units_row // 2

    def finish(part_refs, extra_refs, total, out_refs):
        keep, send = out_refs
        for k in range(half):
            keep[k] = total[k]
            send[k] = total[half + k]
        squares = [ref[quarter] for ref in part_refs]
        square = (squares[0] + squares[1]) + (squares[2] + squares[3])
        keep[half] = square
        send[half] = square

    return tile_products(
        index, parts, tiles, rows, False, units_col, units_row, finish, [],
        [(half + 1, scen, tile)] * 2,
    )


def right_sides_of(demand_rows, earlier, lead, tile, share):
    scen, rows = demand_rows.shape
    sub = rows // tile

    def body(demand_ref, *refs):
        earlier_refs, lead_ref, out_refs = refs[:LEAD_MAX], refs[LEAD_MAX], refs[LEAD_MAX + 1 :]
        for half, out_ref in enumerate(out_refs):
            own = slice(half * share, (half + 1) * share)
            for k in range(sub):
                lanes = slice(k * tile, (k + 1) * tile)
                wanted = lead_ref[k : k + 1, :]
                lagged = jnp.zeros((share, tile), F32)
                for steps in range(1, LEAD_MAX + 1):
                    earlier_ref = earlier_refs[steps - 1]
                    first = scen if earlier_ref.shape[0] > scen else 0
                    here = slice(first + own.start, first + own.stop)
                    lagged = jnp.where(wanted == steps, earlier_ref[here, lanes], lagged)
                out_ref[k] = demand_ref[own, lanes] - return_share * lagged
            for k in range(sub, 2 * sub + 1):
                out_ref[k] = jnp.zeros((share, tile), F32)

    return call_in_vmem(
        body,
        (demand_rows, *earlier, lead),
        [(2 * sub + 1, share, tile)] * (scen // share),
    )


def next_weight(weight, primal_square, dual_square):
    primal_sum = jnp.sum(primal_square, axis=-1, keepdims=True)
    dual_sum = jnp.sum(dual_square, axis=-1, keepdims=True)
    ratio = (primal_sum + epsilon) / (dual_sum + epsilon)
    return jnp.sqrt(weight * jnp.sqrt(ratio))


def primal_update(own, other, starts, primal, weight, primal_square, rows, sub, last):
    _, scen, tile = own.shape
    cost_row = starts[0].shape[0] - 1
    first = primal is None

    def body(*refs):
        own_ref, other_ref = refs[:2]
        start_refs = refs[2:4]
        weight_ref = refs[4]
        rest = refs[5:]
        if not first:
            primal_ref, square_ref = rest[:2]
            rest = rest[2:]
        new_ref, message = rest[:2]
        rest = rest[2:]
        weight_now = weight_ref[...]
        if not first:
            weight_now = next_weight(
                weight_now, square_ref[...], own_ref[2 * sub] + other_ref[2 * sub]
            )
            rest[0][...] = weight_now
            rest = rest[1:]
        primal_step = step_scale / weight_now
        squares = []
        for chunk in range(2):
            square = jnp.zeros((scen, tile), F32)
            for k in range(sub):
                here = chunk * sub + k
                lanes = slice(k * tile, (k + 1) * tile)
                pull = own_ref[here] + other_ref[(1 - chunk) * sub + k]
                before = start_refs[chunk][rows, lanes] if first else primal_ref[here]
                cost = start_refs[chunk][cost_row : cost_row + 1, lanes]
                after = jnp.maximum(before - primal_step * (cost - pull), 0.0)
                change = after - before
                square = square + change * change
                new_ref[here] = after
                message[here] = 2.0 * after - before
                if last and chunk == 0:
                    rest[0][:, lanes] = after
            squares.append(square)
        message[2 * sub] = squares[0] + squares[1]

    inputs = [own, other, *starts, weight]
    outputs = [(2 * sub, scen, tile), (2 * sub + 1, scen, tile)]
    if not first:
        inputs += [primal, primal_square]
        outputs.append((scen, tile))
    if last:
        outputs.append((scen, sub * tile))
    return call_in_vmem(body, inputs, outputs)


def dual_update(own, other, duals, weight, rows, sub, last):
    _, scen, tile = own.shape

    def body(*refs):
        own_ref, other_ref, weight_ref = refs[:3]
        dual_refs = refs[3 : 3 + len(duals)]
        message, square_ref = refs[3 + len(duals) :][:2]
        square_ref[...] = own_ref[2 * sub] + other_ref[2 * sub]
        dual_step = step_scale * weight_ref[...]
        squares = []
        for chunk in range(2):
            square = jnp.zeros((scen, tile), F32)
            for k in range(sub):
                here = chunk * sub + k
                excess = own_ref[here] + other_ref[(1 - chunk) * sub + k]
                if len(duals) == 2:
                    before = unit_of(dual_refs[chunk], k, tile, rows)
                else:
                    before = dual_refs[0][here]
                after = before - dual_step * excess
                change = after - before
                square = square + change * change
                if not last:
                    message[here] = after
                elif chunk == 0:
                    message[:, k * tile : (k + 1) * tile] = after
            squares.append(square)
        square = squares[0] + squares[1]
        if last:
            refs[-1][...] = square
        else:
            message[2 * sub] = square

    if last:
        outputs = [(scen, sub * tile), (scen, tile), (scen, tile)]
    else:
        outputs = [(2 * sub + 1, scen, tile), (scen, tile)]
    return call_in_vmem(body, [own, other, weight, *duals], outputs)


def summed(own, axis, others, masks=(1, 2, 3)):
    got = []
    for mask, value in zip(masks, others):
        got.append(exchanged(value, axis, mask))
    return (own + got[0]) + (got[1] + got[2])


def every_step(
    demand, lead_periods, matrix_tiles, tile_pos, cost_vector, primal_init, dual_init, weight_init
):
    band_bits = bit_count(lax.axis_size("band"))
    assert bit_count(lax.axis_size("col")) == 2 and band_bits >= 3
    matrix_tiles = matrix_tiles.reshape(matrix_tiles.shape[2:])
    positions = tile_pos.reshape(-1)
    tile = matrix_tiles.shape[-1]
    block_rows, scen = demand.shape
    sub = block_rows // tile
    units_col = sub << band_bits
    units_row = 4 * sub
    order = tuple(range(2, band_bits))

    row_unit, column_unit = positions // units_col, positions % units_col
    apart = (row_unit // sub) ^ lax.axis_index("col")
    row_place = ((apart & 1) * 2 + (apart >> 1)) * sub + row_unit % sub
    apart = (column_unit // sub) ^ lax.axis_index("band")
    column_place = (
        (apart & 3) * (units_col // 4) + bit_position(apart, order) * sub + column_unit % sub
    )
    index = jnp.concatenate([row_place, column_place])

    demand_rows, dual_rows, primal_rows = demand.T, dual_init.T, primal_init.T
    dual_pair = [dual_rows, exchanged(dual_rows, "col", 2)]
    together = lax.axis_size("band") == 2 * LEAD_MAX and 1 << order[-1] == LEAD_MAX
    earlier = []
    for steps in range(1, LEAD_MAX + 1 - together):
        earlier.append(passed_along(demand_rows, "band", steps))
    plain_tiles, turned_tiles, start_rows = prepared(
        matrix_tiles, [primal_rows] + [demand_rows] * together + [cost_vector[None, :]]
    )
    dual_pair += [exchanged(value, "col", 1) for value in dual_pair]
    start_rows = [start_rows, exchanged(start_rows, "band", 1 << order[-1])]
    if together:
        earlier.append(start_rows[1])
    share = scen // STREAMS
    right_sides = right_sides_of(demand_rows, earlier, lead_periods.reshape(sub, tile), tile, share)
    states = []
    for stream in range(STREAMS):
        rows = slice(stream * share, (stream + 1) * share)
        states.append(
            dict(
                rows=rows,
                parts=dual_pair,
                duals=dual_pair[:2],
                weight=jnp.broadcast_to(weight_init[rows, None], (share, tile)),
                primal=None,
                primal_square=None,
                right_side=right_sides[stream],
            )
        )

    def step_of(state, iteration):
        last = iteration == ITERS - 1
        rows = state["rows"]
        pieces = backward_product(index, state["parts"], plain_tiles, rows, units_row, units_col)
        total = summed(pieces[0], "band", pieces[1:])
        for bit in order[:-1]:
            half = total.shape[0] // 2
            send = jnp.concatenate([total[half:-1], total[-1:]])
            total = jnp.concatenate([total[:half], total[-1:]]) + exchanged(send, "band", 1 << bit)
        other = exchanged(total, "band", 1 << order[-1])
        results = primal_update(
            total, other, start_rows, state["primal"], state["weight"],
            state["primal_square"], rows, sub, last,
        )
        state["primal"], ahead = results[:2]
        if iteration:
            state["weight"] = results[2]
        if last:
            state["primal_rows"] = results[-1]
        for bit in order[-2::-1]:
            got = exchanged(ahead, "band", 1 << bit)
            ahead = jnp.concatenate([ahead[:-1], got[:-1], ahead[-1:] + got[-1:]])
        ahead = [ahead]
        for mask in range(1, 4):
            ahead.append(exchanged(ahead[0], "band", mask))
        keep, send = forward_product(index, ahead, turned_tiles, rows, units_row, units_col)
        total = (keep + exchanged(send, "col", 1)) - state["right_side"]
        other = exchanged(total, "col", 2)
        results = dual_update(total, other, state["duals"], state["weight"], rows, sub, last)
        state["primal_square"] = results[1]
        if last:
            state["dual_rows"], _, state["square"] = results
        else:
            state["duals"] = [results[0]]
            state["parts"] = [results[0], exchanged(results[0], "col", 1)]

    for iteration in range(ITERS):
        for state in states:
            step_of(state, iteration)

    def joined(name):
        return jnp.concatenate([state[name] for state in states])

    square = joined("square")
    cols = lax.axis_size("col")
    square = summed(square, ("band", "col"), [square] * 3, (1, cols, cols + 1))
    for bit in range(1, band_bits):
        square = square + exchanged(square, "band", 1 << bit)
    weight = next_weight(joined("weight"), joined("primal_square"), square)[:, 0]
    return (joined("primal_rows").T, joined("dual_rows").T, weight)


def solution(mesh):
    in_specs = (
        P(("band", "col"), None),
        P(("band", "col")),
        P("band", "col", None, None, None),
        P("band", "col", None),
        P(("band", "col")),
        P(("band", "col"), None),
        P(("band", "col"), None),
        P(),
    )
    out_specs = (P(("band", "col"), None), P(("band", "col"), None), P())
    return jax.shard_map(
        every_step, mesh=mesh, in_specs=in_specs, out_specs=out_specs, check_vma=False
    )
```

```python
import math

import jax
import jax.numpy as jnp
from jax import lax
from jax.experimental import pallas as pl
from jax.experimental.pallas import tpu as pltpu
from jax.sharding import PartitionSpec as P


ITERS = 3
LEAD_MAX = 4
GROUP = 128
PIECE = 8
AHEAD = 16
STREAMS = 2
KERNEL_VMEM = 1 << 20

step_scale = 0.45
return_share = 0.6
epsilon = 1e-06
F32 = jnp.float32
BF16 = jnp.bfloat16


def bit_count(count):
    bits = count.bit_length() - 1
    assert count == 1 << bits and bits >= 2
    return bits


def bit_position(relative, order):
    bits = len(order)
    place = 0
    for step, bit in enumerate(order):
        place = place + (((relative >> bit) & 1) << (bits - 1 - step))
    return place


def exchanged(value, axis, mask):
    count = lax.axis_size(axis)
    return lax.ppermute(value, axis, [(source, source ^ mask) for source in range(count)])


def passed_along(value, axis, steps):
    count = lax.axis_size(axis)
    return lax.ppermute(value, axis, [(source, (source + steps) % count) for source in range(count)])


def halves(value):
    high = value.astype(BF16)
    low = (value - high.astype(F32)).astype(BF16)
    return high, low


def stacked(value):
    high, low = halves(value)
    return jnp.concatenate(
        [jnp.concatenate([high, high], 1), jnp.concatenate([low, low], 1)], 0
    )


def in_vmem(array):
    return pltpu.with_memory_space_constraint(array, pltpu.VMEM)


def call_in_vmem(body, inputs, outputs, scratch=(), index=None):
    spec = pl.BlockSpec(memory_space=pltpu.VMEM)
    first = [] if index is None else [index]
    room = KERNEL_VMEM + sum(math.prod(ref.shape) * ref.dtype.itemsize for ref in scratch)
    return pl.pallas_call(
        body,
        out_shape=[pltpu.VMEM(shape, F32) for shape in outputs],
        in_specs=[pl.BlockSpec(memory_space=pltpu.SMEM)] * len(first) + [spec] * len(inputs),
        out_specs=[spec] * len(outputs),
        scratch_shapes=list(scratch),
        compiler_params=pltpu.CompilerParams(vmem_limit_bytes=room),
    )(*first, *(in_vmem(array) for array in inputs))


def unit_of(ref, k, tile, rows):
    return ref[rows, k * tile : (k + 1) * tile] if len(ref.shape) == 2 else ref[k]


def prepared(matrix_tiles, message_rows):
    count, tile, _ = matrix_tiles.shape
    heights = [array.shape[0] for array in message_rows]
    piece = min(PIECE, count)
    pieces = count // piece
    ahead = min(AHEAD, pieces)

    def body(tiles_ref, *refs):
        row_refs = refs[: len(heights)]
        plain_ref, turned_ref, start_ref, held, arrived, small = refs[len(heights) :]

        def copy_of(which):
            return pltpu.make_async_copy(
                tiles_ref.at[pl.ds(which * piece, piece)],
                held.at[pl.ds(which * piece, piece)],
                arrived.at[which],
            )

        row_copies = [
            pltpu.make_async_copy(
                ref, start_ref.at[pl.ds(sum(heights[:which]), heights[which])], small.at[which]
            )
            for which, ref in enumerate(row_refs)
        ]
        for which in range(ahead):
            copy_of(which).start()
        for copy in row_copies:
            copy.start()

        def one_piece(which, carry):
            @pl.when(which + ahead < pieces)
            def _():
                copy_of(which + ahead).start()

            copy_of(which).wait()
            for k in range(piece):
                t = which * piece + k
                high, low = halves(held[t])
                plain_ref[t, :tile] = high
                plain_ref[t, tile:] = low
                turned_ref[t, :tile] = high.T
                turned_ref[t, tile:] = low.T
            return carry

        lax.fori_loop(0, pieces, one_piece, 0)
        for copy in row_copies:
            copy.wait()

    anywhere = pl.BlockSpec(memory_space=pl.ANY)
    spec = pl.BlockSpec(memory_space=pltpu.VMEM)
    in_hbm = [
        pltpu.with_memory_space_constraint(array, pltpu.HBM)
        for array in (matrix_tiles, *message_rows)
    ]
    return pl.pallas_call(
        body,
        out_shape=[
            pltpu.VMEM((count, 2 * tile, tile), BF16),
            pltpu.VMEM((count, 2 * tile, tile), BF16),
            pltpu.VMEM((sum(heights), message_rows[0].shape[1]), F32),
        ],
        in_specs=[anywhere] * len(in_hbm),
        out_specs=[spec] * 3,
        scratch_shapes=[
            pltpu.VMEM((count, tile, tile), F32),
            pltpu.SemaphoreType.DMA((pieces,)),
            pltpu.SemaphoreType.DMA((len(heights),)),
        ],
        compiler_params=pltpu.CompilerParams(
            vmem_limit_bytes=KERNEL_VMEM + count * tile * tile * 4
        ),
    )(*in_hbm)


def tile_products(index, parts, tiles, rows, from_row, operand_units, total_units, finish, extra, outputs):
    count, _, tile = tiles.shape
    scen = rows.stop - rows.start
    group = min(GROUP, count)
    given = len(parts) + len(extra)

    def body(index_ref, tiles_ref, *refs):
        part_refs = refs[: len(parts)]
        extra_refs = refs[len(parts) : given]
        out_refs = refs[given:-2]
        total, operand = refs[-2:]
        total[...] = jnp.zeros_like(total)
        per_part = operand_units // len(parts)
        for which, ref in enumerate(part_refs):
            for k in range(per_part):
                operand[which * per_part + k] = stacked(unit_of(ref, k, tile, rows))

        def one_group(step, carry):
            for k in range(group):
                t = step * group + k
                row = index_ref[t]
                column = index_ref[count + t]
                source, target = (row, column) if from_row else (column, row)
                product = jnp.dot(operand[source], tiles_ref[t], preferred_element_type=F32)
                total[target] += product[:scen] + product[scen:]
            return carry

        lax.fori_loop(0, count // group, one_group, 0)
        finish(part_refs, extra_refs, total, out_refs)

    return call_in_vmem(
        body,
        [tiles, *parts, *extra],
        outputs,
        [
            pltpu.VMEM((total_units, scen, tile), F32),
            pltpu.VMEM((operand_units, 2 * scen, 2 * tile), BF16),
        ],
        index,
    )


def backward_product(index, parts, tiles, rows, units_row, units_col):
    scen, tile = rows.stop - rows.start, tiles.shape[-1]
    quarter = units_col // 4
    carried = len(parts) == 2

    def finish(part_refs, extra_refs, total, out_refs):
        for mask in range(4):
            for k in range(quarter):
                out_refs[mask][k] = total[mask * quarter + k]
        if carried:
            square = part_refs[0][units_row // 2] + part_refs[1][units_row // 2]
        else:
            square = jnp.zeros((scen, tile), F32)
        for mask in range(4):
            out_refs[mask][quarter] = square

    return tile_products(
        index, parts, tiles, rows, True, units_row, units_col, finish, [],
        [(quarter + 1, scen, tile)] * 4,
    )


def forward_product(index, parts, tiles, rows, units_row, units_col):
    _, scen, tile = parts[0].shape
    quarter = units_col // 4
    half = units_row // 2

    def finish(part_refs, extra_refs, total, out_refs):
        keep, send = out_refs
        for k in range(half):
            keep[k] = total[k]
            send[k] = total[half + k]
        squares = [ref[quarter] for ref in part_refs]
        square = (squares[0] + squares[1]) + (squares[2] + squares[3])
        keep[half] = square
        send[half] = square

    return tile_products(
        index, parts, tiles, rows, False, units_col, units_row, finish, [],
        [(half + 1, scen, tile)] * 2,
    )


def right_sides_of(demand_rows, earlier, lead, tile, share):
    scen, rows = demand_rows.shape
    sub = rows // tile

    def body(demand_ref, *refs):
        earlier_refs, lead_ref, out_refs = refs[:LEAD_MAX], refs[LEAD_MAX], refs[LEAD_MAX + 1 :]
        for half, out_ref in enumerate(out_refs):
            own = slice(half * share, (half + 1) * share)
            for k in range(sub):
                lanes = slice(k * tile, (k + 1) * tile)
                wanted = lead_ref[k : k + 1, :]
                lagged = jnp.zeros((share, tile), F32)
                for steps in range(1, LEAD_MAX + 1):
                    earlier_ref = earlier_refs[steps - 1]
                    first = scen if earlier_ref.shape[0] > scen else 0
                    here = slice(first + own.start, first + own.stop)
                    lagged = jnp.where(wanted == steps, earlier_ref[here, lanes], lagged)
                out_ref[k] = demand_ref[own, lanes] - return_share * lagged
            for k in range(sub, 2 * sub + 1):
                out_ref[k] = jnp.zeros((share, tile), F32)

    return call_in_vmem(
        body,
        (demand_rows, *earlier, lead),
        [(2 * sub + 1, share, tile)] * (scen // share),
    )


def next_weight(weight, primal_square, dual_square):
    primal_sum = jnp.sum(primal_square, axis=-1, keepdims=True)
    dual_sum = jnp.sum(dual_square, axis=-1, keepdims=True)
    ratio = (primal_sum + epsilon) / (dual_sum + epsilon)
    return jnp.sqrt(weight * jnp.sqrt(ratio))


def primal_update(own, other, starts, primal, weight, primal_square, rows, sub, last):
    _, scen, tile = own.shape
    cost_row = starts[0].shape[0] - 1
    first = primal is None

    def body(*refs):
        own_ref, other_ref = refs[:2]
        start_refs = refs[2:4]
        weight_ref = refs[4]
        rest = refs[5:]
        if not first:
            primal_ref, square_ref = rest[:2]
            rest = rest[2:]
        message = rest[0]
        rest = rest[1:]
        weight_now = weight_ref[...]
        if not first:
            weight_now = next_weight(
                weight_now, square_ref[...], own_ref[2 * sub] + other_ref[2 * sub]
            )
            rest[0][...] = weight_now
            rest = rest[1:]
        primal_step = step_scale / weight_now
        squares = []
        for chunk in range(2):
            square = jnp.zeros((scen, tile), F32)
            for k in range(sub):
                here = chunk * sub + k
                lanes = slice(k * tile, (k + 1) * tile)
                pull = own_ref[here] + other_ref[(1 - chunk) * sub + k]
                before = start_refs[chunk][rows, lanes] if first else primal_ref[here]
                cost = start_refs[chunk][cost_row : cost_row + 1, lanes]
                after = jnp.maximum(before - primal_step * (cost - pull), 0.0)
                change = after - before
                square = square + change * change
                message[here] = 2.0 * after - before
                if not last:
                    rest[0][here] = after
                elif chunk == 0:
                    rest[0][:, lanes] = after
            squares.append(square)
        message[2 * sub] = squares[0] + squares[1]

    inputs = [own, other, *starts, weight]
    outputs = [(2 * sub + 1, scen, tile)]
    if not first:
        inputs += [primal, primal_square]
        outputs.append((scen, tile))
    outputs.append((scen, sub * tile) if last else (2 * sub, scen, tile))
    return call_in_vmem(body, inputs, outputs)


def dual_update(own, other, duals, weight, rows, sub, last):
    _, scen, tile = own.shape

    def body(*refs):
        own_ref, other_ref, weight_ref = refs[:3]
        dual_refs = refs[3 : 3 + len(duals)]
        message, square_ref = refs[3 + len(duals) :][:2]
        square_ref[...] = own_ref[2 * sub] + other_ref[2 * sub]
        dual_step = step_scale * weight_ref[...]
        squares = []
        for chunk in range(2):
            square = jnp.zeros((scen, tile), F32)
            for k in range(sub):
                here = chunk * sub + k
                excess = own_ref[here] + other_ref[(1 - chunk) * sub + k]
                if len(duals) == 2:
                    before = unit_of(dual_refs[chunk], k, tile, rows)
                else:
                    before = dual_refs[0][here]
                after = before - dual_step * excess
                change = after - before
                square = square + change * change
                if not last:
                    message[here] = after
                elif chunk == 0:
                    message[:, k * tile : (k + 1) * tile] = after
            squares.append(square)
        square = squares[0] + squares[1]
        if last:
            refs[-1][...] = square
        else:
            message[2 * sub] = square

    if last:
        outputs = [(scen, sub * tile), (scen, tile), (scen, tile)]
    else:
        outputs = [(2 * sub + 1, scen, tile), (scen, tile)]
    return call_in_vmem(body, [own, other, weight, *duals], outputs)


def summed(own, axis, others, masks=(1, 2, 3)):
    got = []
    for mask, value in zip(masks, others):
        got.append(exchanged(value, axis, mask))
    return (own + got[0]) + (got[1] + got[2])


def every_step(
    demand, lead_periods, matrix_tiles, tile_pos, cost_vector, primal_init, dual_init, weight_init
):
    band_bits = bit_count(lax.axis_size("band"))
    assert bit_count(lax.axis_size("col")) == 2 and band_bits >= 3
    matrix_tiles = matrix_tiles.reshape(matrix_tiles.shape[2:])
    positions = tile_pos.reshape(-1)
    tile = matrix_tiles.shape[-1]
    block_rows, scen = demand.shape
    sub = block_rows // tile
    units_col = sub << band_bits
    units_row = 4 * sub
    order = tuple(range(2, band_bits))

    row_unit, column_unit = positions // units_col, positions % units_col
    apart = (row_unit // sub) ^ lax.axis_index("col")
    row_place = ((apart & 1) * 2 + (apart >> 1)) * sub + row_unit % sub
    apart = (column_unit // sub) ^ lax.axis_index("band")
    column_place = (
        (apart & 3) * (units_col // 4) + bit_position(apart, order) * sub + column_unit % sub
    )
    index = jnp.concatenate([row_place, column_place])

    demand_rows, dual_rows, primal_rows = demand.T, dual_init.T, primal_init.T
    dual_pair = [dual_rows, exchanged(dual_rows, "col", 2)]
    together = lax.axis_size("band") == 2 * LEAD_MAX and 1 << order[-1] == LEAD_MAX
    earlier = []
    for steps in range(1, LEAD_MAX + 1 - together):
        earlier.append(passed_along(demand_rows, "band", steps))
    plain_tiles, turned_tiles, start_rows = prepared(
        matrix_tiles, [primal_rows] + [demand_rows] * together + [cost_vector[None, :]]
    )
    dual_pair += [exchanged(value, "col", 1) for value in dual_pair]
    start_rows = [start_rows, exchanged(start_rows, "band", 1 << order[-1])]
    if together:
        earlier.append(start_rows[1])
    share = scen // STREAMS
    right_sides = right_sides_of(demand_rows, earlier, lead_periods.reshape(sub, tile), tile, share)
    states = []
    for stream in range(STREAMS):
        rows = slice(stream * share, (stream + 1) * share)
        states.append(
            dict(
                rows=rows,
                parts=dual_pair,
                duals=dual_pair[:2],
                weight=jnp.broadcast_to(weight_init[rows, None], (share, tile)),
                primal=None,
                primal_square=None,
                right_side=right_sides[stream],
            )
        )

    def step_of(state, iteration):
        last = iteration == ITERS - 1
        rows = state["rows"]
        pieces = backward_product(index, state["parts"], plain_tiles, rows, units_row, units_col)
        total = summed(pieces[0], "band", pieces[1:])
        for bit in order[:-1]:
            half = total.shape[0] // 2
            send = jnp.concatenate([total[half:-1], total[-1:]])
            total = jnp.concatenate([total[:half], total[-1:]]) + exchanged(send, "band", 1 << bit)
        other = exchanged(total, "band", 1 << order[-1])
        results = primal_update(
            total, other, start_rows, state["primal"], state["weight"],
            state["primal_square"], rows, sub, last,
        )
        ahead = results[0]
        if iteration:
            state["weight"] = results[1]
        state["primal_rows" if last else "primal"] = results[-1]
        for bit in order[-2::-1]:
            got = exchanged(ahead, "band", 1 << bit)
            ahead = jnp.concatenate([ahead[:-1], got[:-1], ahead[-1:] + got[-1:]])
        ahead = [ahead]
        for mask in range(1, 4):
            ahead.append(exchanged(ahead[0], "band", mask))
        keep, send = forward_product(index, ahead, turned_tiles, rows, units_row, units_col)
        total = (keep + exchanged(send, "col", 1)) - state["right_side"]
        other = exchanged(total, "col", 2)
        results = dual_update(total, other, state["duals"], state["weight"], rows, sub, last)
        state["primal_square"] = results[1]
        if last:
            state["dual_rows"], _, state["square"] = results
        else:
            state["duals"] = [results[0]]
            state["parts"] = [results[0], exchanged(results[0], "col", 1)]

    for iteration in range(ITERS):
        for state in states:
            step_of(state, iteration)

    def joined(name):
        return jnp.concatenate([state[name] for state in states])

    square = joined("square")
    cols = lax.axis_size("col")
    square = summed(square, ("band", "col"), [square] * 3, (1, cols, cols + 1))
    for bit in range(1, band_bits):
        square = square + exchanged(square, "band", 1 << bit)
    weight = next_weight(joined("weight"), joined("primal_square"), square)[:, 0]
    return (joined("primal_rows").T, joined("dual_rows").T, weight)


def solution(mesh):
    in_specs = (
        P(("band", "col"), None),
        P(("band", "col")),
        P("band", "col", None, None, None),
        P("band", "col", None),
        P(("band", "col")),
        P(("band", "col"), None),
        P(("band", "col"), None),
        P(),
    )
    out_specs = (P(("band", "col"), None), P(("band", "col"), None), P())
    return jax.shard_map(
        every_step, mesh=mesh, in_specs=in_specs, out_specs=out_specs, check_vma=False
    )
```

```python
import math

import jax
import jax.numpy as jnp
from jax import lax
from jax.experimental import pallas as pl
from jax.experimental.pallas import tpu as pltpu
from jax.sharding import PartitionSpec as P


ITERS = 3
LEAD_MAX = 4
GROUP = 128
PIECE = 16
AHEAD = 16
STREAMS = 2
KERNEL_VMEM = 1 << 20

step_scale = 0.45
return_share = 0.6
epsilon = 1e-06
F32 = jnp.float32
BF16 = jnp.bfloat16


def bit_count(count):
    bits = count.bit_length() - 1
    assert count == 1 << bits and bits >= 2
    return bits


def bit_position(relative, order):
    bits = len(order)
    place = 0
    for step, bit in enumerate(order):
        place = place + (((relative >> bit) & 1) << (bits - 1 - step))
    return place


def exchanged(value, axis, mask):
    count = lax.axis_size(axis)
    return lax.ppermute(value, axis, [(source, source ^ mask) for source in range(count)])


def passed_along(value, axis, steps):
    count = lax.axis_size(axis)
    return lax.ppermute(value, axis, [(source, (source + steps) % count) for source in range(count)])


def halves(value):
    high = value.astype(BF16)
    low = (value - high.astype(F32)).astype(BF16)
    return high, low


def stacked(value):
    high, low = halves(value)
    return jnp.concatenate(
        [jnp.concatenate([high, high], 1), jnp.concatenate([low, low], 1)], 0
    )


def in_vmem(array):
    return pltpu.with_memory_space_constraint(array, pltpu.VMEM)


def call_in_vmem(body, inputs, outputs, scratch=(), index=None):
    spec = pl.BlockSpec(memory_space=pltpu.VMEM)
    first = [] if index is None else [index]
    room = KERNEL_VMEM + sum(math.prod(ref.shape) * ref.dtype.itemsize for ref in scratch)
    return pl.pallas_call(
        body,
        out_shape=[pltpu.VMEM(shape, F32) for shape in outputs],
        in_specs=[pl.BlockSpec(memory_space=pltpu.SMEM)] * len(first) + [spec] * len(inputs),
        out_specs=[spec] * len(outputs),
        scratch_shapes=list(scratch),
        compiler_params=pltpu.CompilerParams(vmem_limit_bytes=room),
    )(*first, *(in_vmem(array) for array in inputs))


def unit_of(ref, k, tile, rows):
    return ref[rows, k * tile : (k + 1) * tile] if len(ref.shape) == 2 else ref[k]


def prepared(matrix_tiles, message_rows):
    count, tile, _ = matrix_tiles.shape
    heights = [array.shape[0] for array in message_rows]
    piece = min(PIECE, count)
    pieces = count // piece
    ahead = min(AHEAD, pieces)

    def body(tiles_ref, *refs):
        row_refs = refs[: len(heights)]
        plain_ref, turned_ref, start_ref, held, arrived, small = refs[len(heights) :]

        def copy_of(which):
            return pltpu.make_async_copy(
                tiles_ref.at[pl.ds(which * piece, piece)],
                held.at[pl.ds(which * piece, piece)],
                arrived.at[which],
            )

        row_copies = [
            pltpu.make_async_copy(
                ref, start_ref.at[pl.ds(sum(heights[:which]), heights[which])], small.at[which]
            )
            for which, ref in enumerate(row_refs)
        ]
        for which in range(ahead):
            copy_of(which).start()
        for copy in row_copies:
            copy.start()

        def one_piece(which, carry):
            @pl.when(which + ahead < pieces)
            def _():
                copy_of(which + ahead).start()

            copy_of(which).wait()
            for k in range(piece):
                t = which * piece + k
                high, low = halves(held[t])
                plain_ref[t, :tile] = high
                plain_ref[t, tile:] = low
                turned_ref[t, :tile] = high.T
                turned_ref[t, tile:] = low.T
            return carry

        lax.fori_loop(0, pieces, one_piece, 0)
        for copy in row_copies:
            copy.wait()

    anywhere = pl.BlockSpec(memory_space=pl.ANY)
    spec = pl.BlockSpec(memory_space=pltpu.VMEM)
    in_hbm = [
        pltpu.with_memory_space_constraint(array, pltpu.HBM)
        for array in (matrix_tiles, *message_rows)
    ]
    return pl.pallas_call(
        body,
        out_shape=[
            pltpu.VMEM((count, 2 * tile, tile), BF16),
            pltpu.VMEM((count, 2 * tile, tile), BF16),
            pltpu.VMEM((sum(heights), message_rows[0].shape[1]), F32),
        ],
        in_specs=[anywhere] * len(in_hbm),
        out_specs=[spec] * 3,
        scratch_shapes=[
            pltpu.VMEM((count, tile, tile), F32),
            pltpu.SemaphoreType.DMA((pieces,)),
            pltpu.SemaphoreType.DMA((len(heights),)),
        ],
        compiler_params=pltpu.CompilerParams(
            vmem_limit_bytes=KERNEL_VMEM + count * tile * tile * 4
        ),
    )(*in_hbm)


def tile_products(index, parts, tiles, rows, from_row, operand_units, total_units, finish, extra, outputs):
    count, _, tile = tiles.shape
    scen = rows.stop - rows.start
    group = min(GROUP, count)
    given = len(parts) + len(extra)

    def body(index_ref, tiles_ref, *refs):
        part_refs = refs[: len(parts)]
        extra_refs = refs[len(parts) : given]
        out_refs = refs[given:-2]
        total, operand = refs[-2:]
        total[...] = jnp.zeros_like(total)
        per_part = operand_units // len(parts)
        for which, ref in enumerate(part_refs):
            for k in range(per_part):
                operand[which * per_part + k] = stacked(unit_of(ref, k, tile, rows))

        def one_group(step, carry):
            for k in range(group):
                t = step * group + k
                row = index_ref[t]
                column = index_ref[count + t]
                source, target = (row, column) if from_row else (column, row)
                product = jnp.dot(operand[source], tiles_ref[t], preferred_element_type=F32)
                total[target] += product[:scen] + product[scen:]
            return carry

        lax.fori_loop(0, count // group, one_group, 0)
        finish(part_refs, extra_refs, total, out_refs)

    return call_in_vmem(
        body,
        [tiles, *parts, *extra],
        outputs,
        [
            pltpu.VMEM((total_units, scen, tile), F32),
            pltpu.VMEM((operand_units, 2 * scen, 2 * tile), BF16),
        ],
        index,
    )


def backward_product(index, parts, tiles, rows, units_row, units_col):
    scen, tile = rows.stop - rows.start, tiles.shape[-1]
    quarter = units_col // 4
    carried = len(parts) == 2

    def finish(part_refs, extra_refs, total, out_refs):
        for mask in range(4):
            for k in range(quarter):
                out_refs[mask][k] = total[mask * quarter + k]
        if carried:
            square = part_refs[0][units_row // 2] + part_refs[1][units_row // 2]
        else:
            square = jnp.zeros((scen, tile), F32)
        for mask in range(4):
            out_refs[mask][quarter] = square

    return tile_products(
        index, parts, tiles, rows, True, units_row, units_col, finish, [],
        [(quarter + 1, scen, tile)] * 4,
    )


def forward_product(index, parts, tiles, rows, units_row, units_col):
    _, scen, tile = parts[0].shape
    quarter = units_col // 4
    half = units_row // 2

    def finish(part_refs, extra_refs, total, out_refs):
        keep, send = out_refs
        for k in range(half):
            keep[k] = total[k]
            send[k] = total[half + k]
        squares = [ref[quarter] for ref in part_refs]
        square = (squares[0] + squares[1]) + (squares[2] + squares[3])
        keep[half] = square
        send[half] = square

    return tile_products(
        index, parts, tiles, rows, False, units_col, units_row, finish, [],
        [(half + 1, scen, tile)] * 2,
    )


def right_sides_of(demand_rows, earlier, lead, tile, share):
    scen, rows = demand_rows.shape
    sub = rows // tile

    def body(demand_ref, *refs):
        earlier_refs, lead_ref, out_refs = refs[:LEAD_MAX], refs[LEAD_MAX], refs[LEAD_MAX + 1 :]
        for half, out_ref in enumerate(out_refs):
            own = slice(half * share, (half + 1) * share)
            for k in range(sub):
                lanes = slice(k * tile, (k + 1) * tile)
                wanted = lead_ref[k : k + 1, :]
                lagged = jnp.zeros((share, tile), F32)
                for steps in range(1, LEAD_MAX + 1):
                    earlier_ref = earlier_refs[steps - 1]
                    first = scen if earlier_ref.shape[0] > scen else 0
                    here = slice(first + own.start, first + own.stop)
                    lagged = jnp.where(wanted == steps, earlier_ref[here, lanes], lagged)
                out_ref[k] = demand_ref[own, lanes] - return_share * lagged
            for k in range(sub, 2 * sub + 1):
                out_ref[k] = jnp.zeros((share, tile), F32)

    return call_in_vmem(
        body,
        (demand_rows, *earlier, lead),
        [(2 * sub + 1, share, tile)] * (scen // share),
    )


def next_weight(weight, primal_square, dual_square):
    primal_sum = jnp.sum(primal_square, axis=-1, keepdims=True)
    dual_sum = jnp.sum(dual_square, axis=-1, keepdims=True)
    ratio = (primal_sum + epsilon) / (dual_sum + epsilon)
    return jnp.sqrt(weight * jnp.sqrt(ratio))


def primal_update(own, other, starts, primal, weight, primal_square, rows, sub, last):
    _, scen, tile = own.shape
    cost_row = starts[0].shape[0] - 1
    first = primal is None

    def body(*refs):
        own_ref, other_ref = refs[:2]
        start_refs = refs[2:4]
        weight_ref = refs[4]
        rest = refs[5:]
        if not first:
            primal_ref, square_ref = rest[:2]
            rest = rest[2:]
        message = rest[0]
        rest = rest[1:]
        weight_now = weight_ref[...]
        if not first:
            weight_now = next_weight(
                weight_now, square_ref[...], own_ref[2 * sub] + other_ref[2 * sub]
            )
            rest[0][...] = weight_now
            rest = rest[1:]
        primal_step = step_scale / weight_now
        squares = []
        for chunk in range(2):
            square = jnp.zeros((scen, tile), F32)
            for k in range(sub):
                here = chunk * sub + k
                lanes = slice(k * tile, (k + 1) * tile)
                pull = own_ref[here] + other_ref[(1 - chunk) * sub + k]
                before = start_refs[chunk][rows, lanes] if first else primal_ref[here]
                cost = start_refs[chunk][cost_row : cost_row + 1, lanes]
                after = jnp.maximum(before - primal_step * (cost - pull), 0.0)
                change = after - before
                square = square + change * change
                message[here] = 2.0 * after - before
                if not last:
                    rest[0][here] = after
                elif chunk == 0:
                    rest[0][:, lanes] = after
            squares.append(square)
        message[2 * sub] = squares[0] + squares[1]

    inputs = [own, other, *starts, weight]
    outputs = [(2 * sub + 1, scen, tile)]
    if not first:
        inputs += [primal, primal_square]
        outputs.append((scen, tile))
    outputs.append((scen, sub * tile) if last else (2 * sub, scen, tile))
    return call_in_vmem(body, inputs, outputs)


def dual_update(own, other, duals, weight, rows, sub, last):
    _, scen, tile = own.shape

    def body(*refs):
        own_ref, other_ref, weight_ref = refs[:3]
        dual_refs = refs[3 : 3 + len(duals)]
        message, square_ref = refs[3 + len(duals) :][:2]
        square_ref[...] = own_ref[2 * sub] + other_ref[2 * sub]
        dual_step = step_scale * weight_ref[...]
        squares = []
        for chunk in range(2):
            square = jnp.zeros((scen, tile), F32)
            for k in range(sub):
                here = chunk * sub + k
                excess = own_ref[here] + other_ref[(1 - chunk) * sub + k]
                if len(duals) == 2:
                    before = unit_of(dual_refs[chunk], k, tile, rows)
                else:
                    before = dual_refs[0][here]
                after = before - dual_step * excess
                change = after - before
                square = square + change * change
                if not last:
                    message[here] = after
                elif chunk == 0:
                    message[:, k * tile : (k + 1) * tile] = after
            squares.append(square)
        square = squares[0] + squares[1]
        if last:
            refs[-1][...] = square
        else:
            message[2 * sub] = square

    if last:
        outputs = [(scen, sub * tile), (scen, tile), (scen, tile)]
    else:
        outputs = [(2 * sub + 1, scen, tile), (scen, tile)]
    return call_in_vmem(body, [own, other, weight, *duals], outputs)


def summed(own, axis, others, masks=(1, 2, 3)):
    got = []
    for mask, value in zip(masks, others):
        got.append(exchanged(value, axis, mask))
    return (own + got[0]) + (got[1] + got[2])


def every_step(
    demand, lead_periods, matrix_tiles, tile_pos, cost_vector, primal_init, dual_init, weight_init
):
    band_bits = bit_count(lax.axis_size("band"))
    assert bit_count(lax.axis_size("col")) == 2 and band_bits >= 3
    matrix_tiles = matrix_tiles.reshape(matrix_tiles.shape[2:])
    positions = tile_pos.reshape(-1)
    tile = matrix_tiles.shape[-1]
    block_rows, scen = demand.shape
    sub = block_rows // tile
    units_col = sub << band_bits
    units_row = 4 * sub
    order = tuple(range(2, band_bits))

    row_unit, column_unit = positions // units_col, positions % units_col
    apart = (row_unit // sub) ^ lax.axis_index("col")
    row_place = ((apart & 1) * 2 + (apart >> 1)) * sub + row_unit % sub
    apart = (column_unit // sub) ^ lax.axis_index("band")
    column_place = (
        (apart & 3) * (units_col // 4) + bit_position(apart, order) * sub + column_unit % sub
    )
    index = jnp.concatenate([row_place, column_place])

    demand_rows, dual_rows, primal_rows = demand.T, dual_init.T, primal_init.T
    dual_pair = [dual_rows, exchanged(dual_rows, "col", 2)]
    together = lax.axis_size("band") == 2 * LEAD_MAX and 1 << order[-1] == LEAD_MAX
    earlier = []
    for steps in range(1, LEAD_MAX + 1 - together):
        earlier.append(passed_along(demand_rows, "band", steps))
    plain_tiles, turned_tiles, start_rows = prepared(
        matrix_tiles, [primal_rows] + [demand_rows] * together + [cost_vector[None, :]]
    )
    dual_pair += [exchanged(value, "col", 1) for value in dual_pair]
    start_rows = [start_rows, exchanged(start_rows, "band", 1 << order[-1])]
    if together:
        earlier.append(start_rows[1])
    share = scen // STREAMS
    right_sides = right_sides_of(demand_rows, earlier, lead_periods.reshape(sub, tile), tile, share)
    states = []
    for stream in range(STREAMS):
        rows = slice(stream * share, (stream + 1) * share)
        states.append(
            dict(
                rows=rows,
                parts=dual_pair,
                duals=dual_pair[:2],
                weight=jnp.broadcast_to(weight_init[rows, None], (share, tile)),
                primal=None,
                primal_square=None,
                right_side=right_sides[stream],
            )
        )

    def step_of(state, iteration):
        last = iteration == ITERS - 1
        rows = state["rows"]
        pieces = backward_product(index, state["parts"], plain_tiles, rows, units_row, units_col)
        total = summed(pieces[0], "band", pieces[1:])
        for bit in order[:-1]:
            half = total.shape[0] // 2
            send = jnp.concatenate([total[half:-1], total[-1:]])
            total = jnp.concatenate([total[:half], total[-1:]]) + exchanged(send, "band", 1 << bit)
        other = exchanged(total, "band", 1 << order[-1])
        results = primal_update(
            total, other, start_rows, state["primal"], state["weight"],
            state["primal_square"], rows, sub, last,
        )
        ahead = results[0]
        if iteration:
            state["weight"] = results[1]
        state["primal_rows" if last else "primal"] = results[-1]
        for bit in order[-2::-1]:
            got = exchanged(ahead, "band", 1 << bit)
            ahead = jnp.concatenate([ahead[:-1], got[:-1], ahead[-1:] + got[-1:]])
        ahead = [ahead]
        for mask in range(1, 4):
            ahead.append(exchanged(ahead[0], "band", mask))
        keep, send = forward_product(index, ahead, turned_tiles, rows, units_row, units_col)
        total = (keep + exchanged(send, "col", 1)) - state["right_side"]
        other = exchanged(total, "col", 2)
        results = dual_update(total, other, state["duals"], state["weight"], rows, sub, last)
        state["primal_square"] = results[1]
        if last:
            state["dual_rows"], _, state["square"] = results
        else:
            state["duals"] = [results[0]]
            state["parts"] = [results[0], exchanged(results[0], "col", 1)]

    for iteration in range(ITERS):
        for state in states:
            step_of(state, iteration)

    def joined(name):
        return jnp.concatenate([state[name] for state in states])

    square = joined("square")
    cols = lax.axis_size("col")
    square = summed(square, ("band", "col"), [square] * 3, (1, cols, cols + 1))
    square = summed(square, "band", [square] * 3, (2, 4, 6))
    for bit in range(3, band_bits):
        square = square + exchanged(square, "band", 1 << bit)
    weight = next_weight(joined("weight"), joined("primal_square"), square)[:, 0]
    return (joined("primal_rows").T, joined("dual_rows").T, weight)


def solution(mesh):
    in_specs = (
        P(("band", "col"), None),
        P(("band", "col")),
        P("band", "col", None, None, None),
        P("band", "col", None),
        P(("band", "col")),
        P(("band", "col"), None),
        P(("band", "col"), None),
        P(),
    )
    out_specs = (P(("band", "col"), None), P(("band", "col"), None), P())
    return jax.shard_map(
        every_step, mesh=mesh, in_specs=in_specs, out_specs=out_specs, check_vma=False
    )
```
